256 devices in a mesh: dp: 16 (over z, y_hi), tensor: 16 (over y_lo, x, core).
Axes of the slice: x: 4, y: 4 (y_hi: 2, y_lo: 2; y = y_hi * 2 + y_lo), z: 8, core: 2. Of those that a mesh axis runs over, the one named last changes fastest.
Arguments:
- picture_averaged_encodings: bfloat16 [12288, 1152], P('dp'), may hold values from -6 to 6
- caption_averaged_encodings: bfloat16 [12288, 1152], P('dp'), may hold values from -6 to 6
- picture_mapping_matrix: bfloat16 [1152, 1152], P(None, 'tensor'), may hold values from -0.1875 to 0.1875
- caption_mapping_matrix: bfloat16 [1152, 1152], P(None, 'tensor'), may hold values from -0.1875 to 0.1875
- picture_weight_perturbation: bfloat16 [1152, 1152], P(None, 'tensor'), may hold values from -0.1875 to 0.1875
- caption_weight_perturbation: bfloat16 [1152, 1152], P(None, 'tensor'), may hold values from -0.1875 to 0.1875
- sharpness_multiplier: float32 [1], replicated, may hold values from 6 to 14
- offset_additive: float32 [1], replicated, may hold values from -8 to -4
Outputs:
- image_hvp: float32 [1152, 1152], P('dp', 'tensor')
- text_hvp: float32 [1152, 1152], P('dp', 'tensor')
The draws below stay inside these ranges and needn't reach their ends.
All inputs are finite; a program needn't handle non-finite values.
Results may differ from the reference program's by a relative error of at most 0.0025.
Values may be sent and summed in bfloat16 or wider, within the bound.
A program may use at most 128 MiB of HBM per device.

```python
import jax
import jax.numpy as jnp
from jax import lax

D = 1152
PAIRS = 12288
N_DP = 16


def levels(rng, shape, shards, low, top_value):
    def one(position, parts):
        heights = jax.random.uniform(jax.random.fold_in(jax.random.fold_in(rng, 6), position), (parts,), jnp.float32, low / len(shards), top_value / len(shards))
        return jnp.repeat(jnp.exp(heights), shape[position] // parts).reshape((-1,) + (1,) * (len(shape) - position - 1))

    factor_of = one(*shards[0])
    for cut in shards[1:]:
        factor_of = factor_of * one(*cut)
    return factor_of


def normal_values(own_key, extent, scale, bound, pieces=(), held_as=jnp.bfloat16):
    array = jax.random.normal(own_key, extent, jnp.float32) * scale
    if len(pieces) > 0:
        array = levels(own_key, extent, pieces, -0.22, 0.18) * array
    return jnp.clip(array, min=-bound, max=bound).astype(held_as)


def setup_inputs(seed: int = 0) -> dict:
    key_list = jax.random.split(jax.random.key(seed), 9)
    return {
        "picture_averaged_encodings": normal_values(key_list[0], (PAIRS, D), 1.0, 6.0, ((0, 16),)),
        "caption_averaged_encodings": normal_values(key_list[1], (PAIRS, D), 1.0, 6.0, ((0, 16),)),
        "picture_mapping_matrix": normal_values(key_list[2], (D, D), D ** -0.5, 0.1875, ((1, 16),)),
        "caption_mapping_matrix": normal_values(key_list[3], (D, D), D ** -0.5, 0.1875, ((1, 16),)),
        "picture_weight_perturbation": normal_values(key_list[4], (D, D), D ** -0.5, 0.1875, ((1, 16),)),
        "caption_weight_perturbation": normal_values(key_list[5], (D, D), D ** -0.5, 0.1875, ((1, 16),)),
        "sharpness_multiplier": jnp.clip(jax.random.uniform(key_list[6], (1,), jnp.float32, 6.0, 14.0), 6.0, 14.0),
        "offset_additive": jnp.clip(jax.random.uniform(key_list[7], (1,), jnp.float32, -8.0, -4.0), -8.0, -4.0),
    }


EPS = 1e-06

def matmul(left, right):
    return jnp.dot(left, right, preferred_element_type=jnp.float32)

def matmul_nt(left, right):
    return lax.dot_general(left, right, (((1,), (1,)), ((), ())), preferred_element_type=jnp.float32)

def matmul_tn(left, right):
    return lax.dot_general(left, right, (((0,), (0,)), ((), ())), preferred_element_type=jnp.float32)

def unit_parts(raw, raw_rate):
    values = raw.astype(jnp.float32)
    tangent = raw_rate.astype(jnp.float32)
    radius = jnp.sqrt(lax.optimization_barrier(jnp.sum(values * values, axis=1, keepdims=True)) + EPS)
    unit = values / radius
    rate = lax.optimization_barrier(jnp.sum(unit * tangent, axis=1, keepdims=True))
    unit_tangent = (tangent - unit * rate) / radius
    return (unit, unit_tangent, radius, rate)

def unit_backward(unit, unit_tangent, radius, rate, grad, grad_rate):
    inner = lax.optimization_barrier(jnp.sum(unit * grad, axis=1, keepdims=True))
    inner_rate = lax.optimization_barrier(jnp.sum(unit_tangent * grad + unit * grad_rate, axis=1, keepdims=True))
    first = (grad - unit * inner) / radius
    return (grad_rate - unit_tangent * inner - unit * inner_rate - first * rate) / radius

def reference(picture_averaged_encodings, caption_averaged_encodings, picture_mapping_matrix, caption_mapping_matrix, picture_weight_perturbation, caption_weight_perturbation, sharpness_multiplier, offset_additive):
    similarity_multiplier = sharpness_multiplier[0]
    logit_bias = offset_additive[0]
    image_raw = matmul(picture_averaged_encodings, picture_mapping_matrix).astype(jnp.bfloat16)
    image_raw_rate = matmul(picture_averaged_encodings, picture_weight_perturbation).astype(jnp.bfloat16)
    text_raw = matmul(caption_averaged_encodings, caption_mapping_matrix).astype(jnp.bfloat16)
    text_raw_rate = matmul(caption_averaged_encodings, caption_weight_perturbation).astype(jnp.bfloat16)
    image_unit, image_tangent, image_radius, image_rate = unit_parts(image_raw, image_raw_rate)
    text_unit, text_tangent, text_radius, text_rate = unit_parts(text_raw, text_raw_rate)
    image_half = image_unit.astype(jnp.bfloat16)
    image_tangent_half = image_tangent.astype(jnp.bfloat16)
    text_half = text_unit.astype(jnp.bfloat16)
    text_tangent_half = text_tangent.astype(jnp.bfloat16)
    total = picture_averaged_encodings.shape[0]
    block_rows = total // N_DP

    def visit(carry, block_index):
        text_grad, text_grad_rate = carry
        start = (block_index * block_rows).astype(jnp.int32)
        rows_unit = lax.dynamic_slice_in_dim(image_half, start, block_rows, 0)
        rows_tangent = lax.dynamic_slice_in_dim(image_tangent_half, start, block_rows, 0)
        logits = similarity_multiplier * matmul_nt(rows_unit, text_half) + logit_bias
        logit_rate = similarity_multiplier * (matmul_nt(rows_tangent, text_half) + matmul_nt(rows_unit, text_tangent_half))
        probability = jax.nn.sigmoid(logits)
        row_ids = lax.broadcasted_iota(jnp.int32, (block_rows, 1), 0) + start
        col_ids = lax.broadcasted_iota(jnp.int32, (1, total), 1)
        positive = (row_ids == col_ids).astype(jnp.float32)
        weight = (probability - positive).astype(jnp.bfloat16)
        weight_rate = (probability * (1.0 - probability) * logit_rate).astype(jnp.bfloat16)
        image_grad = similarity_multiplier * matmul(weight, text_half)
        image_grad_rate = similarity_multiplier * (matmul(weight_rate, text_half) + matmul(weight, text_tangent_half))
        text_grad = text_grad + similarity_multiplier * matmul_tn(weight, rows_unit)
        text_grad_rate = text_grad_rate + similarity_multiplier * (matmul_tn(weight_rate, rows_unit) + matmul_tn(weight, rows_tangent))
        return ((text_grad, text_grad_rate), (image_grad, image_grad_rate))
    empty_rows = jnp.zeros((total, picture_mapping_matrix.shape[1]), jnp.float32)
    carried, stacked = lax.scan(visit, (empty_rows, empty_rows), jnp.arange(N_DP, dtype=jnp.int32))
    text_grad, text_grad_rate = carried
    image_grad = stacked[0].reshape(total, -1)
    image_grad_rate = stacked[1].reshape(total, -1)
    image_back = unit_backward(image_unit, image_tangent, image_radius, image_rate, image_grad, image_grad_rate).astype(jnp.bfloat16)
    text_back = unit_backward(text_unit, text_tangent, text_radius, text_rate, text_grad, text_grad_rate).astype(jnp.bfloat16)
    image_hvp = matmul_tn(picture_averaged_encodings, image_back)
    text_hvp = matmul_tn(caption_averaged_encodings, text_back)
    return (image_hvp, text_hvp)
```

```python
import functools

import jax
import jax.numpy as jnp
from jax import lax
from jax.experimental import pallas as pl
from jax.experimental.pallas import tpu as pltpu
from jax.sharding import PartitionSpec as P

EPS = 1e-06
MESH = pl.DeviceIdType.MESH
F32 = jnp.float32
BF16 = jnp.bfloat16

DP_SLOTS = (
    (True, 0), (False, 0), (True, 1), (True, -1),
    (False, 1), (False, -1), (True, 2), (True, -2),
    (False, 2), (False, -2), (True, 3), (True, -3),
    (False, 3), (False, -3), (True, 4), (False, -4),
)
TP_CHIPS = (
    (True, 0), (False, 0), (True, 1), (True, -1),
    (False, 1), (False, -1), (True, 2), (False, -2),
)
TP_SLOTS = tuple((y, x, c) for y, x in TP_CHIPS for c in (True, False))


def mirror(slots, period):
    found = []
    for slot in slots:
        back = (slot[0], -slot[1]) + tuple(slot[2:])
        if back not in slots:
            back = (slot[0], slot[1]) + tuple(slot[2:])
            assert 2 * abs(slot[1]) == period
        found.append(slots.index(back))
    return tuple(found)


def dot_nn(a, b):
    return lax.dot_general(a, b, (((1,), (0,)), ((), ())), preferred_element_type=F32)


def dot_nt(a, b):
    return lax.dot_general(a, b, (((1,), (1,)), ((), ())), preferred_element_type=F32)


def dot_tn(a, b):
    return lax.dot_general(a, b, (((0,), (0,)), ((), ())), preferred_element_type=F32)


def split_hi(value):
    hi = value.astype(BF16)
    lo = (value - hi.astype(F32)).astype(BF16)
    return hi, lo


def lanes_of(values, rows):
    lane = lax.broadcasted_iota(jnp.int32, (rows, 128), 1)
    out = jnp.zeros((rows, 128), F32)
    for index, value in enumerate(values):
        out = jnp.where(lane == index, value.astype(F32), out)
    return out


def kernel(
    nz, nx, D, W,
    enc_i, enc_t, w_i, w_t, dw_i, dw_t, scalars,
    out_i, out_t,
    wpad, x_buf, x_got, raw, img, txt, gi, pb_buf, at_buf, csum,
    si_buf, st_buf, ri_buf, rt_buf, stage, cols, hv, hv_got,
    fs, fr, ais, air, ats, atr, ris, rir, rts, rtr, bs, br, hs, hr,
):
    dp = lax.axis_index("dp")
    tp = lax.axis_index("tensor")
    z, h = dp // 2, dp % 2
    y, x, c = tp // (2 * nx), (tp // 2) % nx, tp % 2
    rows = enc_i.shape[0]
    share = rows // 16
    DX = D + 128
    DE = 2 * D + 128
    s = scalars[0]
    bias = scalars[1]

    def dp_of(slot):
        same, back = slot
        zz = (z - back + nz) % nz
        hh = h if same else 1 - h
        return zz * 2 + hh

    def tp_of(slot):
        same, back, own = slot
        xx = (x - back + nx) % nx
        yy = y if same else 1 - y
        cc = c if own else 1 - c
        return (yy * nx + xx) * 2 + cc

    dp_ids = [dp_of(q) for q in DP_SLOTS]
    tp_ids = [tp_of(q) for q in TP_SLOTS]
    dp_back = mirror(DP_SLOTS, nz)
    tp_back = mirror(TP_SLOTS, nx)
    d_at = {q: i for i, q in enumerate(DP_SLOTS)}
    t_at = {q: i for i, q in enumerate(TP_SLOTS)}

    started = []

    def send(src, dst, ssem, rsem, device):
        copy = pltpu.make_async_remote_copy(
            src_ref=src, dst_ref=dst, send_sem=ssem, recv_sem=rsem,
            device_id=device, device_id_type=MESH,
        )
        copy.start()
        started.append(copy)

    def arrived(dst, rsem):
        pltpu.make_async_remote_copy(
            src_ref=dst, dst_ref=dst, send_sem=fs.at[0], recv_sem=rsem,
            device_id=(dp, tp), device_id_type=MESH,
        ).wait_recv()

    barrier = pltpu.get_barrier_semaphore()
    for q in range(1, 16):
        pl.semaphore_signal(barrier, inc=1, device_id=(dp_ids[q], tp), device_id_type=MESH)
        pl.semaphore_signal(barrier, inc=1, device_id=(dp, tp_ids[q]), device_id_type=MESH)

    wpad[...] = jnp.zeros_like(wpad)
    wpad[:, 0:W] = w_i[...]
    wpad[:, 128 : 128 + W] = dw_i[...]
    wpad[:, 256 : 256 + W] = w_t[...]
    wpad[:, 384 : 384 + W] = dw_t[...]

    def project(r, carry):
        at = pl.ds(pl.multiple_of(r * 256, 256), 256)
        x_buf[at, 0:256] = dot_nn(enc_i[at, :], wpad[:, 0:256]).astype(BF16)
        x_buf[at, 256:512] = dot_nn(enc_t[at, :], wpad[:, 256:512]).astype(BF16)
        return carry

    lax.fori_loop(0, rows // 256, project, 0)
    pl.semaphore_wait(barrier, 30)

    def share_at(index):
        return pl.ds(pl.multiple_of(index * share, share), share)

    for q in range(1, 16):
        send(x_buf.at[share_at(tp_ids[q]), :], x_got.at[tp], fs.at[q], fr.at[tp], (dp, tp_ids[q]))
    x_got[pl.ds(tp, 1)] = x_buf[share_at(tp), :].reshape(1, share, 512)
    for q in range(1, 16):
        arrived(x_got.at[tp_ids[q]], fr.at[tp_ids[q]])
    for q in range(16):
        for k in range(4):
            raw[k, :, q * W : (q + 1) * W] = x_got[q, :, k * 128 : k * 128 + W].astype(F32)

    def unit_parts(values, tangent):
        radius = jnp.sqrt(jnp.sum(values * values, axis=1, keepdims=True) + EPS)
        unit = values / radius
        rate = jnp.sum(unit * tangent, axis=1, keepdims=True)
        unit_tangent = (tangent - unit * rate) / radius
        return unit, unit_tangent, radius, rate / radius

    for k, buf in ((0, img), (2, txt)):
        unit, tangent, radius, ratio = unit_parts(raw[k], raw[k + 1])
        buf[0:share, 0:D] = unit.astype(BF16)
        buf[0:share, D : 2 * D] = tangent.astype(BF16)
        hi, lo = split_hi(ratio)
        buf[0:share, 2 * D : DE] = lanes_of((hi, lo), share).astype(BF16)

    def iat(slot):
        return img.at[pl.ds(slot * share, share), :]

    def tat(slot):
        return txt.at[pl.ds(slot * share, share), :]

    counts = {"i": 0, "t": 0}

    def isend(src, dst, device):
        send(iat(src), iat(dst), ais.at[counts["i"]], air.at[dst], (dp, device))
        counts["i"] += 1

    def tsend(src, dst, device):
        send(tat(src), tat(dst), ats.at[counts["t"]], atr.at[dst], (device, tp))
        counts["t"] += 1

    def iwait(slot):
        arrived(iat(slot), air.at[slot])

    def twait(slot):
        arrived(tat(slot), atr.at[slot])

    sib = tp_ids[t_at[(True, 0, False)]]
    x_right = tp_ids[t_at[(True, -1, True)]]
    x_left = tp_ids[t_at[(True, 1, True)]]
    z_right = dp_ids[d_at[(True, -1)]]
    z_left = dp_ids[d_at[(True, 1)]]

    def t_on(same, back):
        src = d_at[(same, back)]
        if back >= 0 and (same, back + 1) in d_at:
            tsend(src, d_at[(same, back + 1)], z_right)
        if back <= 0 and (same, back - 1) in d_at:
            tsend(src, d_at[(same, back - 1)], z_left)

    def i_on(same, back):
        src = t_at[(same, back, True)]
        if back >= 0 and (same, back + 1, True) in t_at:
            isend(src, t_at[(same, back + 1, True)], x_right)
        if back <= 0 and (same, back - 1, True) in t_at:
            isend(src, t_at[(same, back - 1, True)], x_left)
        isend(src, t_at[(same, back, False)], sib)

    def t_step(same, back):
        twait(d_at[(same, back)])
        t_on(same, back)

    def i_step(same, back):
        iwait(t_at[(same, back, True)])
        i_on(same, back)

    isend(0, t_at[(False, 0, True)], tp_ids[t_at[(False, 0, True)]])
    tsend(0, d_at[(False, 0)], dp_ids[d_at[(False, 0)]])
    i_on(True, 0)
    t_on(True, 0)
    i_step(False, 0)
    t_step(False, 0)
    for back in (1, -1):
        i_step(True, back)
        t_step(True, back)
    for back in (1, -1):
        i_step(False, back)
        t_step(False, back)
    i_step(True, 2)
    i_step(False, -2)
    t_step(True, 2)
    t_step(True, -2)
    for chip in TP_CHIPS:
        iwait(t_at[chip + (False,)])

    eye = lanes_of([(lax.broadcasted_iota(jnp.int32, (8, 1), 0) == k) for k in range(8)], 8).astype(BF16)
    TC = 4 * share
    RB = 256

    def chunk(ci):
        at = pl.ds(ci * TC, TC)
        ends = txt[at, 2 * D : DE].astype(F32)
        sigma = ends[:, 0:1] + ends[:, 1:2]
        csum[...] = jnp.zeros_like(csum)

        def block(r, carry):
            ra = pl.ds(pl.multiple_of(r * RB, RB), RB)
            tu = txt[at, 0:D]
            tt = txt[at, D : 2 * D]
            iu = img[ra, 0:D]
            it = img[ra, D : 2 * D]
            extra = img[ra, 2 * D : DE].astype(F32)
            rho = extra[:, 0:1] + extra[:, 1:2]
            cosine = dot_nt(iu, tu)
            cross = dot_nt(it, tu) + dot_nt(iu, tt)
            prob = jax.nn.sigmoid(s * cosine + bias)
            rate = prob * (1.0 - prob) * (s * cross)
            pb = prob.astype(BF16)
            q1 = prob * cosine
            q2 = prob * cross + rate * cosine
            csum[0:1, :] += jnp.sum(q1, axis=0, keepdims=True)
            csum[1:2, :] += jnp.sum(q2, axis=0, keepdims=True)
            rb = rate.astype(BF16)
            pb_buf[ra, :] = pb
            at_buf[ra, :] = rb
            gain = dot_nn(rb, tu) + dot_nn(pb, tt) - rho * dot_nn(pb, tu)
            sums = lanes_of((jnp.sum(q1, axis=1, keepdims=True), jnp.sum(q2, axis=1, keepdims=True)), RB)
            if ci == 0:
                gi[ra, 0:D] = gain
                gi[ra, D:DX] = sums
            else:
                gi[ra, 0:D] += gain
                gi[ra, D:DX] += sums
            return carry

        lax.fori_loop(0, rows // RB, block, 0)

        hi, lo = split_hi(csum[...])
        tops = jnp.concatenate([hi[0:2].astype(F32), lo[0:2].astype(F32), jnp.zeros((4, TC), F32)], axis=0)
        st_buf[at, D:DX] = dot_tn(tops.astype(BF16), eye).astype(BF16)

        def columns(k, carry):
            ka = pl.ds(pl.multiple_of(k * 384, 128), 384)
            kb = pl.ds(pl.multiple_of(D + k * 384, 128), 384)
            gain = dot_tn(at_buf[...], img[:, ka]) + dot_tn(pb_buf[...], img[:, kb])
            st_buf[at, ka] = (gain - sigma * dot_tn(pb_buf[...], img[:, ka])).astype(BF16)
            return carry

        lax.fori_loop(0, D // 384, columns, 0)
        for q in range(4 * ci, 4 * ci + 4):
            if q > 0:
                k = dp_back[q]
                send(st_buf.at[pl.ds(q * share, share), :], rt_buf.at[k], rts.at[q], rtr.at[k], (dp_ids[q], tp))

    chunk(0)
    for back in (2, -2):
        t_step(False, back)
    t_step(True, 3)
    t_step(True, -3)
    chunk(1)
    t_step(False, -3)
    t_step(False, 3)
    chunk(2)
    t_step(True, 4)
    t_step(False, -4)
    chunk(3)

    for q in range(1, 16):
        qa = pl.ds(q * share, share)
        si_buf[qa, 0:D] = gi[qa, 0:D].astype(BF16)
        hi, lo = split_hi(gi[qa, D:DX])
        hi, lo = hi.astype(F32), lo.astype(F32)
        si_buf[qa, D:DX] = lanes_of((hi[:, 0:1], hi[:, 1:2], lo[:, 0:1], lo[:, 1:2]), share).astype(BF16)
        k = tp_back[q]
        send(si_buf.at[qa, :], ri_buf.at[k], ris.at[q], rir.at[k], (dp, tp_ids[q]))

    for q in range(1, 16):
        arrived(rt_buf.at[q], rtr.at[q])
    for q in range(1, 16):
        arrived(ri_buf.at[q], rir.at[q])

    iu, it = img[0:share, 0:D].astype(F32), img[0:share, D : 2 * D].astype(F32)
    tu, tt = txt[0:share, 0:D].astype(F32), txt[0:share, D : 2 * D].astype(F32)
    pair_cos = jnp.sum(iu * tu, axis=1, keepdims=True)
    pair_cross = jnp.sum(it * tu + iu * tt, axis=1, keepdims=True)
    stage[...] = jnp.zeros_like(stage)
    for k, got in ((0, ri_buf), (1, rt_buf)):
        if k == 0:
            total = gi[0:share, 0:D]
            inner = gi[0:share, D : D + 1]
            inner_rate = gi[0:share, D + 1 : D + 2]
            other, other_tangent = tu, tt
        else:
            total = st_buf[0:share, 0:D].astype(F32)
            own = st_buf[0:share, D:DX].astype(F32)
            inner = own[:, 0:1] + own[:, 2:3]
            inner_rate = own[:, 1:2] + own[:, 3:4]
            other, other_tangent = iu, it
        for q in range(1, 16):
            total = total + got[q, :, 0:D].astype(F32)
            ends = got[q, :, D:DX].astype(F32)
            inner = inner + (ends[:, 0:1] + ends[:, 2:3])
            inner_rate = inner_rate + (ends[:, 1:2] + ends[:, 3:4])
        unit, tangent, radius, ratio = unit_parts(raw[2 * k], raw[2 * k + 1])
        total = s * (total + (ratio * other - other_tangent))
        inner = s * (inner - pair_cos)
        inner_rate = s * (inner_rate - pair_cross)
        raw[2 * k] = (total - tangent * inner - unit * (inner_rate - ratio * inner)) / radius
        for q in range(16):
            hi, lo = split_hi(raw[2 * k, :, q * W : (q + 1) * W])
            stage[q, :, k * 256 : k * 256 + W] = hi
            stage[q, :, k * 256 + 128 : k * 256 + 128 + W] = lo

    for q in range(1, 16):
        send(stage.at[tp_ids[q]], cols.at[share_at(tp), :], bs.at[q], br.at[tp], (dp, tp_ids[q]))
    cols[share_at(tp), :] = stage[pl.ds(tp, 1)].reshape(share, 512)
    for q in range(1, 16):
        arrived(cols.at[share_at(tp_ids[q]), :], br.at[tp_ids[q]])

    def head(k, carry):
        ka = pl.ds(pl.multiple_of(k * 128, 128), 128)
        both = dot_tn(enc_i[:, ka], cols[:, 0:256])
        hv[ka, 0:128] = both[:, 0:128] + both[:, 128:256]
        both = dot_tn(enc_t[:, ka], cols[:, 256:512])
        hv[ka, 128:256] = both[:, 0:128] + both[:, 128:256]
        return carry

    lax.fori_loop(0, D // 128, head, 0)

    def own_rows(index):
        return pl.ds(pl.multiple_of(index * W, 8), W)

    for q in range(1, 16):
        k = dp_back[q]
        send(hv.at[own_rows(dp_ids[q]), :], hv_got.at[k], hs.at[q], hr.at[k], (dp_ids[q], tp))
    total = hv[own_rows(dp), :]
    for q in range(1, 16):
        arrived(hv_got.at[q], hr.at[q])
        total = total + hv_got[q]
    out_i[...] = total[:, 0:W]
    out_t[...] = total[:, 128 : 128 + W]
    for copy in started:
        copy.wait_send()


def solution(mesh):
    nz = mesh.shape["dp"] // 2
    nx = mesh.shape["tensor"] // 4

    def local(enc_i, enc_t, w_i, w_t, dw_i, dw_t, sharpness, offset):
        rows, D = enc_i.shape
        W = w_i.shape[1]
        share = rows // 16
        DX, DE = D + 128, 2 * D + 128
        scalars = jnp.concatenate([sharpness, offset])
        vmem = pl.BlockSpec(memory_space=pltpu.VMEM)
        sem = pltpu.SemaphoreType.DMA((16,))
        return pl.pallas_call(
            functools.partial(kernel, nz, nx, D, W),
            out_shape=[jax.ShapeDtypeStruct((W, W), F32)] * 2,
            in_specs=[vmem] * 6 + [pl.BlockSpec(memory_space=pltpu.SMEM)],
            out_specs=[vmem] * 2,
            scratch_shapes=[
                pltpu.VMEM((D, 512), BF16),
                pltpu.VMEM((rows, 512), BF16),
                pltpu.VMEM((16, share, 512), BF16),
                pltpu.VMEM((4, share, D), F32),
                pltpu.VMEM((rows, DE), BF16),
                pltpu.VMEM((rows, DE), BF16),
                pltpu.VMEM((rows, DX), F32),
                pltpu.VMEM((rows, 4 * share), BF16),
                pltpu.VMEM((rows, 4 * share), BF16),
                pltpu.VMEM((8, 4 * share), F32),
                pltpu.VMEM((rows, DX), BF16),
                pltpu.VMEM((rows, DX), BF16),
                pltpu.VMEM((16, share, DX), BF16),
                pltpu.VMEM((16, share, DX), BF16),
                pltpu.VMEM((16, share, 512), BF16),
                pltpu.VMEM((rows, 512), BF16),
                pltpu.VMEM((D, 256), F32),
                pltpu.VMEM((16, W, 256), F32),
            ]
            + [sem] * 14,
            compiler_params=pltpu.CompilerParams(
                collective_id=0, has_side_effects=True, vmem_limit_bytes=60 * 2**20
            ),
        )(enc_i, enc_t, w_i, w_t, dw_i, dw_t, scalars)

    in_specs = (
        P("dp", None),
        P("dp", None),
        P(None, "tensor"),
        P(None, "tensor"),
        P(None, "tensor"),
        P(None, "tensor"),
        P(),
        P(),
    )
    out_specs = (P("dp", "tensor"), P("dp", "tensor"))
    return jax.shard_map(local, mesh=mesh, in_specs=in_specs, out_specs=out_specs, check_vma=False)
```

```python
import functools

import jax
import jax.numpy as jnp
from jax import lax
from jax.experimental import pallas as pl
from jax.experimental.pallas import tpu as pltpu
from jax.sharding import PartitionSpec as P

EPS = 1e-06
MESH = pl.DeviceIdType.MESH
F32 = jnp.float32
BF16 = jnp.bfloat16

Z_SLOTS = (0, 1, -1, 2, -2, 3, -3, 4)
XY_SLOTS = tuple(
    sorted(((i, j) for i in (0, 1, -1, 2) for j in (0, 1, -1, 2)), key=lambda p: abs(p[0]) + abs(p[1]))
)


def mirrored(back, period):
    return back if 2 * abs(back) == period else -back


def dot_nn(a, b):
    return lax.dot_general(a, b, (((1,), (0,)), ((), ())), preferred_element_type=F32)


def dot_nt(a, b):
    return lax.dot_general(a, b, (((1,), (1,)), ((), ())), preferred_element_type=F32)


def dot_tn(a, b):
    return lax.dot_general(a, b, (((0,), (0,)), ((), ())), preferred_element_type=F32)


def split_hi(value):
    hi = value.astype(BF16)
    lo = (value - hi.astype(F32)).astype(BF16)
    return hi, lo


def lanes_of(values, rows):
    lane = lax.broadcasted_iota(jnp.int32, (rows, 128), 1)
    out = jnp.zeros((rows, 128), F32)
    for index, value in enumerate(values):
        out = jnp.where(lane == index, value.astype(F32), out)
    return out


def kernel(
    nz, nx, D, W,
    enc_i, enc_t, w_i, w_t, dw_i, dw_t, scalars,
    out_i, out_t,
    wpad, x_buf, x_got, raw, img, txt, gi, pb_buf, at_buf, csum,
    si_buf, st_buf, sib_got, ri_buf, rt_buf, stage, cols, hv, hv_got, ent_i, ent_t,
    fs, fr, ais, air, ats, atr, gs, gr, ris, rir, rts, rtr, bs, br, hs, hr,
):
    dp = lax.axis_index("dp")
    tp = lax.axis_index("tensor")
    z, h = dp // 2, dp % 2
    y, x, c = h * 2 + tp // (2 * nx), (tp // 2) % nx, tp % 2
    rows = enc_i.shape[0]
    share = rows // 16
    half = 16 * share
    DX = D + 128
    DE = 2 * D + 128
    s = scalars[0]
    bias = scalars[1]

    def device_at(dz, dy, dx, core):
        zz, yy, xx = (z - dz + nz) % nz, (y - dy + 4) % 4, (x - dx + nx) % nx
        return (zz * 2 + yy // 2, ((yy % 2) * nx + xx) * 2 + core)

    tp_ids = [(tp + q) % 16 for q in range(16)]
    z_ids = [device_at(b, 0, 0, c) for b in Z_SLOTS]
    xy_ids = [device_at(0, dy, dx, c) for dx, dy in XY_SLOTS]
    z_back = [Z_SLOTS.index(mirrored(b, nz)) for b in Z_SLOTS]
    xy_back = [XY_SLOTS.index((mirrored(dx, nx), mirrored(dy, 4))) for dx, dy in XY_SLOTS]

    started = []

    def send(src, dst, ssem, rsem, device):
        copy = pltpu.make_async_remote_copy(
            src_ref=src, dst_ref=dst, send_sem=ssem, recv_sem=rsem,
            device_id=device, device_id_type=MESH,
        )
        copy.start()
        started.append(copy)

    def arrived(dst, rsem):
        pltpu.make_async_remote_copy(
            src_ref=dst, dst_ref=dst, send_sem=fs.at[0], recv_sem=rsem,
            device_id=(dp, tp), device_id_type=MESH,
        ).wait_recv()

    barrier = pltpu.get_barrier_semaphore()
    peers = [(dp, tp_ids[q]) for q in range(1, 16)]
    peers += [(z * 2 + 1 - h, (tp + 2 * q) % 16) for q in range(8)]
    peers += [((dp + q) % 16, tp) for q in range(2, 15)]
    peers += [((dp + 15 - 14 * h) % 16, tp)]
    for peer in peers:
        pl.semaphore_signal(barrier, inc=1, device_id=peer, device_id_type=MESH)

    wpad[...] = jnp.zeros_like(wpad)
    wpad[0:W] = w_i[...]
    wpad[128 : 128 + W] = dw_i[...]
    wpad[256 : 256 + W] = w_t[...]
    wpad[384 : 384 + W] = dw_t[...]

    def project(r, carry):
        at = pl.ds(pl.multiple_of(r * 256, 256), 256)
        x_buf[at, 0:256] = dot_nt(enc_i[at, :], wpad[0:256]).astype(BF16)
        x_buf[at, 256:512] = dot_nt(enc_t[at, :], wpad[256:512]).astype(BF16)
        return carry

    lax.fori_loop(0, rows // 256, project, 0)
    pl.semaphore_wait(barrier, len(peers))

    def share_at(index):
        return pl.ds(pl.multiple_of(index * share, share), share)

    for q in range(1, 16):
        send(x_buf.at[share_at(tp_ids[q]), :], x_got.at[tp], fs.at[q], fr.at[tp], (dp, tp_ids[q]))
    x_got[pl.ds(tp, 1)] = x_buf[share_at(tp), :].reshape(1, share, 512)
    for q in range(1, 16):
        arrived(x_got.at[tp_ids[q]], fr.at[tp_ids[q]])
    for q in range(16):
        for k in range(4):
            raw[k, :, q * W : (q + 1) * W] = x_got[q, :, k * 128 : k * 128 + W].astype(F32)

    def unit_parts(values, tangent):
        radius = jnp.sqrt(jnp.sum(values * values, axis=1, keepdims=True) + EPS)
        unit = values / radius
        rate = jnp.sum(unit * tangent, axis=1, keepdims=True)
        unit_tangent = (tangent - unit * rate) / radius
        return unit, unit_tangent, radius, rate / radius

    for k, buf in ((0, img), (2, txt)):
        unit, tangent, radius, ratio = unit_parts(raw[k], raw[k + 1])
        buf[0:share, 0:D] = unit.astype(BF16)
        buf[0:share, D : 2 * D] = tangent.astype(BF16)
        hi, lo = split_hi(ratio)
        buf[0:share, 2 * D : DE] = lanes_of((hi, lo), share).astype(BF16)

    parts = ((0, D), (D, DE - D))
    counts = {"i": 0, "t": 0}
    sib = (dp, tp + 1 - 2 * c)

    def ipart(slot, part):
        return img.at[pl.ds(slot * share, share), pl.ds(*parts[part])]

    def tat(slot):
        return txt.at[pl.ds(slot * share, share), :]

    def isend(src, dst, part, device):
        send(ipart(src, part), ipart(dst, part), ais.at[counts["i"]], air.at[part * 32 + dst], device)
        counts["i"] += 1

    def hop(pos, axis, way, part):
        to = list(pos)
        to[axis] = 2 if abs(pos[axis] + way) == 2 else pos[axis] + way
        away = [0, 0]
        away[axis] = -way
        isend(XY_SLOTS.index(pos), XY_SLOTS.index(tuple(to)), part, device_at(0, away[1], away[0], c))

    def i_on(pos, part):
        first, second = (0, 1) if part == 0 else (1, 0)
        if pos[second] == 0:
            if pos[first] >= 0 and (pos[first] == 0 or (part == 0 and pos[first] == 1)):
                hop(pos, first, 1, part)
            if pos[first] == 0 or (part == 1 and pos[first] == -1):
                hop(pos, first, -1, part)
            hop(pos, second, 1, part)
            hop(pos, second, -1, part)
        else:
            forth = pos[first] in (0, 2)
            if pos[second] == 1 and forth:
                hop(pos, second, 1, part)
            if pos[second] == -1 and not forth:
                hop(pos, second, -1, part)
        isend(XY_SLOTS.index(pos), 16 + XY_SLOTS.index(pos), part, sib)

    def i_step(pos):
        for part in (0, 1):
            slot = XY_SLOTS.index(pos)
            arrived(ipart(slot, part), air.at[part * 32 + slot])
            i_on(pos, part)

    def tsend(src, dst, device):
        send(tat(src), tat(dst), ats.at[counts["t"]], atr.at[dst], device)
        counts["t"] += 1

    def t_on(back):
        src = Z_SLOTS.index(back)
        if 0 <= back < 3:
            tsend(src, Z_SLOTS.index(back + 1), device_at(-1, 0, 0, c))
        if -3 < back <= 0:
            tsend(src, Z_SLOTS.index(back - 1), device_at(1, 0, 0, c))

    def twait(back):
        slot = Z_SLOTS.index(back)
        arrived(tat(slot), atr.at[slot])

    for part in (0, 1):
        i_on((0, 0), part)
    t_on(0)
    for k in range(D // 128):
        ka = pl.ds(k * 128, 128)
        ent_i[ka, :] = enc_i[:, ka].T
        ent_t[ka, :] = enc_t[:, ka].T
    for pos in XY_SLOTS[1:5]:
        i_step(pos)
    for back in (1, -1):
        twait(back)
        t_on(back)
    for pos in XY_SLOTS[5:11]:
        i_step(pos)
    for back in (2, -2):
        twait(back)
        t_on(back)
    for pos in XY_SLOTS[11:16]:
        i_step(pos)
    for back in (3, -3):
        twait(back)
    far = Z_SLOTS.index(3) + c * (Z_SLOTS.index(-3) - Z_SLOTS.index(3))
    tsend(pl.multiple_of(far, 1), Z_SLOTS.index(4), device_at(2 * c - 1, 0, 0, c))
    for slot in range(16):
        for part in (0, 1):
            arrived(ipart(16 + slot, part), air.at[part * 32 + 16 + slot])

    eye = lanes_of([(lax.broadcasted_iota(jnp.int32, (8, 1), 0) == k) for k in range(8)], 8).astype(BF16)
    TC = 4 * share
    RB = 4 * share

    def chunk(ci, between):
        at = pl.ds(ci * TC, TC)
        ends = txt[at, 2 * D : DE].astype(F32)
        sigma = ends[:, 0:1] + ends[:, 1:2]
        csum[...] = jnp.zeros_like(csum)

        def block(r, carry):
            ra = pl.ds(pl.multiple_of(r * RB, RB), RB)
            tu = txt[at, 0:D]
            tt = txt[at, D : 2 * D]
            iu = img[ra, 0:D]
            it = img[ra, D : 2 * D]
            extra = img[ra, 2 * D : DE].astype(F32)
            rho = extra[:, 0:1] + extra[:, 1:2]
            cosine = dot_nt(iu, tu)
            cross = dot_nt(it, tu) + dot_nt(iu, tt)
            prob = jax.nn.sigmoid(s * cosine + bias)
            rate = prob * (1.0 - prob) * (s * cross)
            pb = prob.astype(BF16)
            q1 = prob * cosine
            q2 = prob * cross + rate * cosine
            csum[0:1, :] += jnp.sum(q1, axis=0, keepdims=True)
            csum[1:2, :] += jnp.sum(q2, axis=0, keepdims=True)
            rb = rate.astype(BF16)
            pb_buf[ra, :] = pb
            at_buf[ra, :] = rb
            gain = dot_nn(rb, tu) + dot_nn(pb, tt) - rho * dot_nn(pb, tu)
            sums = lanes_of((jnp.sum(q1, axis=1, keepdims=True), jnp.sum(q2, axis=1, keepdims=True)), RB)
            if ci == 0:
                gi[ra, 0:D] = gain
                gi[ra, D:DX] = sums
            else:
                gi[ra, 0:D] += gain
                gi[ra, D:DX] += sums
            return carry

        lax.fori_loop(half // RB, 2 * half // RB, block, 0)
        between()
        lax.fori_loop(0, half // RB, block, 0)

        hi, lo = split_hi(csum[...])
        tops = jnp.concatenate([hi[0:2].astype(F32), lo[0:2].astype(F32), jnp.zeros((4, TC), F32)], axis=0)
        st_buf[at, D:DX] = dot_tn(tops.astype(BF16), eye).astype(BF16)

        def columns(k, carry):
            ka = pl.ds(pl.multiple_of(k * 384, 128), 384)
            kb = pl.ds(pl.multiple_of(D + k * 384, 128), 384)
            gain = dot_tn(at_buf[...], img[:, ka]) + dot_tn(pb_buf[...], img[:, kb])
            st_buf[at, ka] = (gain - sigma * dot_tn(pb_buf[...], img[:, ka])).astype(BF16)
            return carry

        lax.fori_loop(0, D // 384, columns, 0)
        for q in range(4 * ci, 4 * ci + 4):
            if q > 0:
                k = z_back[q]
                send(st_buf.at[pl.ds(q * share, share), :], rt_buf.at[k], rts.at[q], rtr.at[k], z_ids[q])

    def sums_out(row, extra):
        at = pl.ds(row, share)
        total, ends = gi[at, 0:D], gi[at, D:DX]
        inner, inner_rate = ends[:, 0:1], ends[:, 1:2]
        if extra is not None:
            total = total + extra[:, 0:D].astype(F32)
            ends = extra[:, D:DX].astype(F32)
            inner = inner + (ends[:, 0:1] + ends[:, 2:3])
            inner_rate = inner_rate + (ends[:, 1:2] + ends[:, 3:4])
        si_buf[at, 0:D] = total.astype(BF16)
        (ih, il), (rh, rl) = split_hi(inner), split_hi(inner_rate)
        si_buf[at, D:DX] = lanes_of((ih, rh, il, rl), share).astype(BF16)

    def nothing():
        pass

    def to_sibling():
        for g in range(4):
            def one(q, carry):
                sums_out(pl.multiple_of(half + (4 * g + q) * share, share), None)
                return carry
            lax.fori_loop(0, 4, one, 0)
            src = si_buf.at[pl.ds(half + 4 * g * share, 4 * share), :]
            send(src, sib_got.at[pl.ds(4 * g * share, 4 * share), :], gs.at[g], gr.at[g], sib)

    chunk(0, nothing)
    twait(4)
    chunk(1, to_sibling)

    for g in range(4):
        arrived(sib_got.at[pl.ds(4 * g * share, 4 * share), :], gr.at[g])
        for q in range(4 * g, 4 * g + 4):
            if q > 0:
                qa = pl.ds(q * share, share)
                sums_out(q * share, sib_got[qa, :])
                k = xy_back[q]
                send(si_buf.at[qa, :], ri_buf.at[k], ris.at[q], rir.at[k], xy_ids[q])

    for q in range(1, 8):
        arrived(rt_buf.at[q], rtr.at[q])
    for q in range(1, 16):
        arrived(ri_buf.at[q], rir.at[q])

    iu, it = img[0:share, 0:D].astype(F32), img[0:share, D : 2 * D].astype(F32)
    tu, tt = txt[0:share, 0:D].astype(F32), txt[0:share, D : 2 * D].astype(F32)
    pair_cos = jnp.sum(iu * tu, axis=1, keepdims=True)
    pair_cross = jnp.sum(it * tu + iu * tt, axis=1, keepdims=True)
    stage[...] = jnp.zeros_like(stage)
    for k, got in ((0, ri_buf), (1, rt_buf)):
        if k == 0:
            total = gi[0:share, 0:D]
            inner = gi[0:share, D : D + 1]
            inner_rate = gi[0:share, D + 1 : D + 2]
            more = [sib_got[0:share, :]] + [got[q] for q in range(1, 16)]
            other, other_tangent = tu, tt
        else:
            total, inner, inner_rate = 0.0, 0.0, 0.0
            more = [st_buf[0:share, :]] + [got[q] for q in range(1, 8)]
            other, other_tangent = iu, it
        for term in more:
            total = total + term[:, 0:D].astype(F32)
            ends = term[:, D:DX].astype(F32)
            inner = inner + (ends[:, 0:1] + ends[:, 2:3])
            inner_rate = inner_rate + (ends[:, 1:2] + ends[:, 3:4])
        unit, tangent, radius, ratio = unit_parts(raw[2 * k], raw[2 * k + 1])
        total = s * (total + (ratio * other - other_tangent))
        inner = s * (inner - pair_cos)
        inner_rate = s * (inner_rate - pair_cross)
        raw[2 * k] = (total - tangent * inner - unit * (inner_rate - ratio * inner)) / radius
        for q in range(16):
            hi, lo = split_hi(raw[2 * k, :, q * W : (q + 1) * W])
            stage[q, :, k * 256 : k * 256 + W] = hi
            stage[q, :, k * 256 + 128 : k * 256 + 128 + W] = lo

    for q in range(1, 16):
        send(stage.at[tp_ids[q]], cols.at[share_at(tp), :], bs.at[q], br.at[tp], (dp, tp_ids[q]))
    cols[share_at(tp), :] = stage[pl.ds(tp, 1)].reshape(share, 512)
    for q in range(1, 16):
        arrived(cols.at[share_at(tp_ids[q]), :], br.at[tp_ids[q]])

    def head(k, carry):
        ka = pl.ds(pl.multiple_of(k * 128, 128), 128)
        both = dot_nn(ent_i[ka, :], cols[:, 0:256])
        hv[ka, 0:128] = both[:, 0:128] + both[:, 128:256]
        both = dot_nn(ent_t[ka, :], cols[:, 256:512])
        hv[ka, 128:256] = both[:, 0:128] + both[:, 128:256]
        return carry

    lax.fori_loop(0, D // 128, head, 0)

    def own_rows(index):
        return pl.ds(pl.multiple_of(index * W, 8), W)

    for q in range(1, 16):
        to = (dp + q) % 16
        send(hv.at[own_rows(to), :], hv_got.at[16 - q], hs.at[q], hr.at[16 - q], (to, tp))
    total = hv[own_rows(dp), :]
    for q in range(1, 16):
        arrived(hv_got.at[q], hr.at[q])
        total = total + hv_got[q]
    out_i[...] = total[:, 0:W]
    out_t[...] = total[:, 128 : 128 + W]
    for copy in started:
        copy.wait_send()


def solution(mesh):
    nz = mesh.shape["dp"] // 2
    nx = mesh.shape["tensor"] // 4

    def local(enc_i, enc_t, w_i, w_t, dw_i, dw_t, sharpness, offset):
        rows, D = enc_i.shape
        W = w_i.shape[1]
        share = rows // 16
        DX, DE = D + 128, 2 * D + 128
        scalars = jnp.concatenate([sharpness, offset])
        vmem = pl.BlockSpec(memory_space=pltpu.VMEM)
        sem = lambda n: pltpu.SemaphoreType.DMA((n,))
        return pl.pallas_call(
            functools.partial(kernel, nz, nx, D, W),
            out_shape=[jax.ShapeDtypeStruct((W, W), F32)] * 2,
            in_specs=[vmem] * 6 + [pl.BlockSpec(memory_space=pltpu.SMEM)],
            out_specs=[vmem] * 2,
            scratch_shapes=[
                pltpu.VMEM((512, D), BF16),
                pltpu.VMEM((rows, 512), BF16),
                pltpu.VMEM((16, share, 512), BF16),
                pltpu.VMEM((4, share, D), F32),
                pltpu.VMEM((32 * share, DE), BF16),
                pltpu.VMEM((8 * share, DE), BF16),
                pltpu.VMEM((32 * share, DX), F32),
                pltpu.VMEM((32 * share, 4 * share), BF16),
                pltpu.VMEM((32 * share, 4 * share), BF16),
                pltpu.VMEM((8, 4 * share), F32),
                pltpu.VMEM((32 * share, DX), BF16),
                pltpu.VMEM((8 * share, DX), BF16),
                pltpu.VMEM((16 * share, DX), BF16),
                pltpu.VMEM((16, share, DX), BF16),
                pltpu.VMEM((8, share, DX), BF16),
                pltpu.VMEM((16, share, 512), BF16),
                pltpu.VMEM((rows, 512), BF16),
                pltpu.VMEM((D, 256), F32),
                pltpu.VMEM((16, W, 256), F32),
                pltpu.VMEM((D, rows), BF16),
                pltpu.VMEM((D, rows), BF16),
            ]
            + [sem(n) for n in (16, 16, 64, 64, 8, 8, 4, 4, 16, 16, 8, 8, 16, 16, 16, 16)],
            compiler_params=pltpu.CompilerParams(
                collective_id=0, has_side_effects=True, vmem_limit_bytes=60 * 2**20
            ),
        )(enc_i, enc_t, w_i.T, w_t.T, dw_i.T, dw_t.T, scalars)

    in_specs = (
        P("dp", None),
        P("dp", None),
        P(None, "tensor"),
        P(None, "tensor"),
        P(None, "tensor"),
        P(None, "tensor"),
        P(),
        P(),
    )
    out_specs = (P("dp", "tensor"), P("dp", "tensor"))
    return jax.shard_map(local, mesh=mesh, in_specs=in_specs, out_specs=out_specs, check_vma=False)
```

```python
import functools

import jax
import jax.numpy as jnp
from jax import lax
from jax.experimental import pallas as pl
from jax.experimental.pallas import tpu as pltpu
from jax.sharding import PartitionSpec as P

EPS = 1e-06
MESH = pl.DeviceIdType.MESH
F32 = jnp.float32
BF16 = jnp.bfloat16

Z_SLOTS = (0, 1, -1, 2, -2, 3, -3, 4)
XY_SLOTS = tuple(
    sorted(((i, j) for i in (0, 1, -1, 2) for j in (0, 1, -1, 2)), key=lambda p: abs(p[0]) + abs(p[1]))
)


def mirrored(back, period):
    return back if 2 * abs(back) == period else -back


def dot_nn(a, b):
    return lax.dot_general(a, b, (((1,), (0,)), ((), ())), preferred_element_type=F32)


def dot_nt(a, b):
    return lax.dot_general(a, b, (((1,), (1,)), ((), ())), preferred_element_type=F32)


def dot_tn(a, b):
    return lax.dot_general(a, b, (((0,), (0,)), ((), ())), preferred_element_type=F32)


def split_hi(value):
    hi = value.astype(BF16)
    lo = (value - hi.astype(F32)).astype(BF16)
    return hi, lo


def lanes_of(values, rows):
    lane = lax.broadcasted_iota(jnp.int32, (rows, 128), 1)
    out = jnp.zeros((rows, 128), F32)
    for index, value in enumerate(values):
        out = jnp.where(lane == index, value.astype(F32), out)
    return out


def kernel(
    nz, nx, D, W,
    enc_i, enc_t, w_i, w_t, dw_i, dw_t, scalars,
    out_i, out_t,
    wpad, x_buf, x_got, raw, img, txt, gi, pb_buf, at_buf, csum,
    si_buf, st_buf, sib_got, ri_buf, rt_buf, stage, tmp, cols, hv, hp, hv_got, ent_i, ent_t,
    fs, fr, ais, air, ats, atr, gs, gr, ris, rir, rts, rtr, bs, br, hs, hr,
):
    dp = lax.axis_index("dp")
    tp = lax.axis_index("tensor")
    z, h = dp // 2, dp % 2
    y, x, c = h * 2 + tp // (2 * nx), (tp // 2) % nx, tp % 2
    rows = enc_i.shape[0]
    share = rows // 16
    half = 16 * share
    DX = D + 128
    DE = 2 * D + 128
    T0 = 80
    T1 = 128 - T0
    T2 = W - T1
    s = scalars[0]
    bias = scalars[1]

    def device_at(dz, dy, dx, core):
        zz, yy, xx = (z - dz + nz) % nz, (y - dy + 4) % 4, (x - dx + nx) % nx
        return (zz * 2 + yy // 2, ((yy % 2) * nx + xx) * 2 + core)

    tp_ids = [(tp + q) % 16 for q in range(16)]
    z_ids = [device_at(b, 0, 0, c) for b in Z_SLOTS]
    xy_ids = [device_at(0, dy, dx, c) for dx, dy in XY_SLOTS]
    z_back = [Z_SLOTS.index(mirrored(b, nz)) for b in Z_SLOTS]
    xy_back = [XY_SLOTS.index((mirrored(dx, nx), mirrored(dy, 4))) for dx, dy in XY_SLOTS]

    started = []

    def send(src, dst, ssem, rsem, device):
        copy = pltpu.make_async_remote_copy(
            src_ref=src, dst_ref=dst, send_sem=ssem, recv_sem=rsem,
            device_id=device, device_id_type=MESH,
        )
        copy.start()
        started.append(copy)

    def arrived(dst, rsem):
        pltpu.make_async_remote_copy(
            src_ref=dst, dst_ref=dst, send_sem=fs.at[0], recv_sem=rsem,
            device_id=(dp, tp), device_id_type=MESH,
        ).wait_recv()

    barrier = pltpu.get_barrier_semaphore()
    peers = [(dp, tp_ids[q]) for q in range(1, 16)]
    peers += [(z * 2 + 1 - h, (tp + 2 * q) % 16) for q in range(8)]
    peers += [((dp + q) % 16, tp) for q in range(2, 15)]
    peers += [((dp + 15 - 14 * h) % 16, tp)]
    for peer in peers:
        pl.semaphore_signal(barrier, inc=1, device_id=peer, device_id_type=MESH)

    wpad[...] = jnp.zeros_like(wpad)
    wpad[0:W] = w_i[...]
    wpad[128 : 128 + W] = dw_i[...]
    wpad[256 + T0 : 384] = w_t[0:T1]
    wpad[384 + T0 : 512] = dw_t[0:T1]
    wpad[512 : 512 + T2] = w_t[T1:W]
    wpad[544 : 544 + T2] = dw_t[T1:W]

    def project(r, carry):
        at = pl.ds(pl.multiple_of(r * 256, 256), 256)
        text = enc_t[at, :]
        x_buf[at, 0:256] = (dot_nt(enc_i[at, :], wpad[0:256]) + dot_nt(text, wpad[256:512])).astype(BF16)
        x_buf[at, 256:384] = dot_nt(text, wpad[512:640]).astype(BF16)
        return carry

    lax.fori_loop(0, rows // 256, project, 0)
    pl.semaphore_wait(barrier, len(peers))

    def share_at(index):
        return pl.ds(pl.multiple_of(index * share, share), share)

    for q in range(1, 16):
        send(x_buf.at[share_at(tp_ids[q]), :], x_got.at[tp], fs.at[q], fr.at[tp], (dp, tp_ids[q]))
    x_got[pl.ds(tp, 1)] = x_buf[share_at(tp), :].reshape(1, share, 384)
    for q in range(1, 16):
        arrived(x_got.at[tp_ids[q]], fr.at[tp_ids[q]])
    for q in range(16):
        last = x_got[q, :, 256:384].astype(F32)
        for k in range(2):
            tile = x_got[q, :, k * 128 : k * 128 + 128].astype(F32)
            raw[k, :, q * W : (q + 1) * W] = tile[:, 0:W]
            raw[2 + k, :, q * W : q * W + T1] = pltpu.roll(tile, T1, 1)[:, 0:T1]
            rest = last if k == 0 else pltpu.roll(last, 96, 1)
            raw[2 + k, :, q * W + T1 : (q + 1) * W] = rest[:, 0:T2]

    def unit_parts(values, tangent):
        radius = jnp.sqrt(jnp.sum(values * values, axis=1, keepdims=True) + EPS)
        unit = values / radius
        rate = jnp.sum(unit * tangent, axis=1, keepdims=True)
        unit_tangent = (tangent - unit * rate) / radius
        return unit, unit_tangent, radius, rate / radius

    for k, buf in ((0, img), (2, txt)):
        unit, tangent, radius, ratio = unit_parts(raw[k], raw[k + 1])
        buf[0:share, 0:D] = unit.astype(BF16)
        buf[0:share, D : 2 * D] = tangent.astype(BF16)
        hi, lo = split_hi(ratio)
        buf[0:share, 2 * D : DE] = lanes_of((hi, lo), share).astype(BF16)

    parts = ((0, D), (D, DE - D))
    counts = {"i": 0, "t": 0}
    sib = (dp, tp + 1 - 2 * c)

    def ipart(slot, part):
        return img.at[pl.ds(slot * share, share), pl.ds(*parts[part])]

    def tat(slot):
        return txt.at[pl.ds(slot * share, share), :]

    def isend(src, dst, part, device):
        send(ipart(src, part), ipart(dst, part), ais.at[counts["i"]], air.at[part * 32 + dst], device)
        counts["i"] += 1

    def hop(pos, axis, way, part):
        to = list(pos)
        to[axis] = 2 if abs(pos[axis] + way) == 2 else pos[axis] + way
        away = [0, 0]
        away[axis] = -way
        isend(XY_SLOTS.index(pos), XY_SLOTS.index(tuple(to)), part, device_at(0, away[1], away[0], c))

    def i_on(pos, part):
        first, second = (0, 1) if part == 0 else (1, 0)
        if pos[second] == 0:
            if pos[first] >= 0 and (pos[first] == 0 or (part == 0 and pos[first] == 1)):
                hop(pos, first, 1, part)
            if pos[first] == 0 or (part == 1 and pos[first] == -1):
                hop(pos, first, -1, part)
            hop(pos, second, 1, part)
            hop(pos, second, -1, part)
        else:
            forth = pos[first] in (0, 2)
            if pos[second] == 1 and forth:
                hop(pos, second, 1, part)
            if pos[second] == -1 and not forth:
                hop(pos, second, -1, part)
        isend(XY_SLOTS.index(pos), 16 + XY_SLOTS.index(pos), part, sib)

    def i_step(pos):
        for part in (0, 1):
            slot = XY_SLOTS.index(pos)
            arrived(ipart(slot, part), air.at[part * 32 + slot])
            i_on(pos, part)

    def tsend(src, dst, device):
        send(tat(src), tat(dst), ats.at[counts["t"]], atr.at[dst], device)
        counts["t"] += 1

    def t_on(back):
        src = Z_SLOTS.index(back)
        if 0 <= back < 3:
            tsend(src, Z_SLOTS.index(back + 1), device_at(-1, 0, 0, c))
        if -3 < back <= 0:
            tsend(src, Z_SLOTS.index(back - 1), device_at(1, 0, 0, c))

    def twait(back):
        slot = Z_SLOTS.index(back)
        arrived(tat(slot), atr.at[slot])

    for part in (0, 1):
        i_on((0, 0), part)
    t_on(0)
    for k in range(D // 128):
        ka = pl.ds(k * 128, 128)
        ent_i[ka, :] = enc_i[:, ka].T
        ent_t[ka, :] = enc_t[:, ka].T
    eye = lanes_of([(lax.broadcasted_iota(jnp.int32, (8, 1), 0) == k) for k in range(8)], 8).astype(BF16)
    first_two = jnp.where(lax.broadcasted_iota(jnp.int32, (8, 128), 1) < 2, 1.0, 0.0).astype(BF16)
    TC = 4 * share
    RB = 8 * share

    def prepare(ci):
        csum[...] = jnp.zeros_like(csum)
        return dot_nt(first_two, txt[ci * TC : (ci + 1) * TC, 2 * D : DE])[0:1, :]

    def blocks(ci, sigma, low, high):
        at = pl.ds(ci * TC, TC)

        def block(r, carry):
            ra = pl.ds(pl.multiple_of(r * RB, RB), RB)
            tu = txt[at, 0:D]
            tt = txt[at, D : 2 * D]
            iu = img[ra, 0:D]
            it = img[ra, D : 2 * D]
            extra = img[ra, 2 * D : DE].astype(F32)
            rho = extra[:, 0:1] + extra[:, 1:2]
            cosine = dot_nt(iu, tu)
            cross = dot_nt(it, tu) + dot_nt(iu, tt)
            prob = jax.nn.sigmoid(s * cosine + bias)
            rate = prob * (1.0 - prob) * (s * cross)
            pb = prob.astype(BF16)
            q1 = prob * cosine
            q2 = prob * cross + rate * cosine
            csum[0:1, :] += jnp.sum(q1, axis=0, keepdims=True)
            csum[1:2, :] += jnp.sum(q2, axis=0, keepdims=True)
            pb_buf[ra, :] = pb
            at_buf[ra, :] = (rate - sigma * prob).astype(BF16)
            gain = dot_nn((rate - rho * prob).astype(BF16), tu) + dot_nn(pb, tt)
            sums = lanes_of((jnp.sum(q1, axis=1, keepdims=True), jnp.sum(q2, axis=1, keepdims=True)), RB)
            if ci == 0:
                gi[ra, 0:D] = gain
                gi[ra, D:DX] = sums
            else:
                gi[ra, 0:D] += gain
                gi[ra, D:DX] += sums
            return carry

        lax.fori_loop(low, high, block, 0)

    def text_sums(ci):
        at = pl.ds(ci * TC, TC)
        hi, lo = split_hi(csum[...])
        tops = jnp.concatenate([hi[0:2].astype(F32), lo[0:2].astype(F32), jnp.zeros((4, TC), F32)], axis=0)
        st_buf[at, D:DX] = dot_tn(tops.astype(BF16), eye).astype(BF16)
        for k in range(0, D, 256):
            e = min(k + 256, D)
            gain = dot_tn(at_buf[...], img[:, k:e]) + dot_tn(pb_buf[...], img[:, D + k : D + e])
            st_buf[at, k:e] = gain.astype(BF16)
        for q in range(4 * ci, 4 * ci + 4):
            if q > 0:
                k = z_back[q]
                send(st_buf.at[pl.ds(q * share, share), :], rt_buf.at[k], rts.at[q], rtr.at[k], z_ids[q])

    def sums_out(row, extra):
        at = pl.ds(row, share)
        total, ends = gi[at, 0:D], gi[at, D:DX]
        inner, inner_rate = ends[:, 0:1], ends[:, 1:2]
        if extra is not None:
            total = total + extra[:, 0:D].astype(F32)
            ends = extra[:, D:DX].astype(F32)
            inner = inner + (ends[:, 0:1] + ends[:, 2:3])
            inner_rate = inner_rate + (ends[:, 1:2] + ends[:, 3:4])
        si_buf[at, 0:D] = total.astype(BF16)
        (ih, il), (rh, rl) = split_hi(inner), split_hi(inner_rate)
        si_buf[at, D:DX] = lanes_of((ih, rh, il, rl), share).astype(BF16)

    def to_sibling():
        for g in range(4):
            def one(q, carry):
                sums_out(pl.multiple_of(half + (4 * g + q) * share, share), None)
                return carry
            lax.fori_loop(0, 4, one, 0)
            src = si_buf.at[pl.ds(half + 4 * g * share, 4 * share), :]
            send(src, sib_got.at[pl.ds(4 * g * share, 4 * share), :], gs.at[g], gr.at[g], sib)

    for pos in XY_SLOTS[1:5]:
        i_step(pos)
    for back in (1, -1):
        twait(back)
        t_on(back)
    for pos in XY_SLOTS[5:8]:
        i_step(pos)
    twait(2)
    t_on(2)
    sigma = prepare(0)
    blocks(0, sigma, 0, 1)
    for pos in XY_SLOTS[8:11]:
        i_step(pos)
    twait(-2)
    t_on(-2)
    for pos in XY_SLOTS[11:16]:
        i_step(pos)
    blocks(0, sigma, 1, 2)
    for back in (3, -3):
        twait(back)
    far = Z_SLOTS.index(3) + c * (Z_SLOTS.index(-3) - Z_SLOTS.index(3))
    tsend(far, Z_SLOTS.index(4), device_at(2 * c - 1, 0, 0, c))
    for slot in range(16):
        for part in (0, 1):
            arrived(ipart(16 + slot, part), air.at[part * 32 + 16 + slot])
    blocks(0, sigma, 2, 4)
    text_sums(0)
    twait(4)
    sigma = prepare(1)
    blocks(1, sigma, 2, 4)
    to_sibling()
    blocks(1, sigma, 0, 2)

    for g in range(4):
        arrived(sib_got.at[pl.ds(4 * g * share, 4 * share), :], gr.at[g])
        for q in range(4 * g, 4 * g + 4):
            if q > 0:
                qa = pl.ds(q * share, share)
                sums_out(q * share, sib_got[qa, :])
                k = xy_back[q]
                send(si_buf.at[qa, :], ri_buf.at[k], ris.at[q], rir.at[k], xy_ids[q])
    text_sums(1)

    for q in range(1, 8):
        arrived(rt_buf.at[q], rtr.at[q])
    for q in range(1, 16):
        arrived(ri_buf.at[q], rir.at[q])

    iu, it = img[0:share, 0:D].astype(F32), img[0:share, D : 2 * D].astype(F32)
    tu, tt = txt[0:share, 0:D].astype(F32), txt[0:share, D : 2 * D].astype(F32)
    pair_cos = jnp.sum(iu * tu, axis=1, keepdims=True)
    pair_cross = jnp.sum(it * tu + iu * tt, axis=1, keepdims=True)
    tmp[...] = jnp.zeros_like(tmp)
    for k, got in ((0, ri_buf), (1, rt_buf)):
        if k == 0:
            total = gi[0:share, 0:D]
            inner = gi[0:share, D : D + 1]
            inner_rate = gi[0:share, D + 1 : D + 2]
            more = [sib_got[0:share, :]] + [got[q] for q in range(1, 16)]
            other, other_tangent = tu, tt
        else:
            total, inner, inner_rate = 0.0, 0.0, 0.0
            more = [st_buf[0:share, :]] + [got[q] for q in range(1, 8)]
            other, other_tangent = iu, it
        for term in more:
            total = total + term[:, 0:D].astype(F32)
            ends = term[:, D:DX].astype(F32)
            inner = inner + (ends[:, 0:1] + ends[:, 2:3])
            inner_rate = inner_rate + (ends[:, 1:2] + ends[:, 3:4])
        unit, tangent, radius, ratio = unit_parts(raw[2 * k], raw[2 * k + 1])
        total = s * (total + (ratio * other - other_tangent))
        inner = s * (inner - pair_cos)
        inner_rate = s * (inner_rate - pair_cross)
        back = (total - tangent * inner - unit * (inner_rate - ratio * inner)) / radius
        hi, lo = split_hi(back)
        raw[2 * k] = hi.astype(F32)
        raw[2 * k + 1] = lo.astype(F32)
    for q in range(16):
        for k in range(2):
            tmp[:, k * 128 : k * 128 + W] = raw[k, :, q * W : (q + 1) * W]
            tmp[:, k * 128 + T0 : k * 128 + 128] = raw[2 + k, :, q * W : q * W + T1]
            tmp[:, 256 + 32 * k : 256 + 32 * k + T2] = raw[2 + k, :, q * W + T1 : (q + 1) * W]
        stage[q] = tmp[...].astype(BF16)

    for q in range(1, 16):
        send(stage.at[tp_ids[q]], cols.at[share_at(tp), :], bs.at[q], br.at[tp], (dp, tp_ids[q]))
    cols[share_at(tp), :] = stage[pl.ds(tp, 1)].reshape(share, 384)
    for q in range(1, 16):
        arrived(cols.at[share_at(tp_ids[q]), :], br.at[tp_ids[q]])

    lane = lax.broadcasted_iota(jnp.int32, (8, 128), 1)
    text_lane = lax.broadcasted_iota(jnp.int32, (128, 128), 1) >= T0

    def head(k, carry):
        ka = pl.ds(pl.multiple_of(k * 128, 128), 128)
        of_i = dot_nn(ent_i[ka, :], cols[:, 0:256])
        of_t = dot_nn(ent_t[ka, :], cols[...])
        hv[ka, 0:128] = jnp.where(text_lane, of_t[:, 0:128] + of_t[:, 128:256], of_i[:, 0:128] + of_i[:, 128:256])
        rest = of_t[:, 256:384]
        hv[ka, 128:256] = rest + pltpu.roll(rest, 96, 1)
        return carry

    lax.fori_loop(0, D // 128, head, 0)

    per = 128 // T2
    places = [(W + 8 * (j // per), T2 * (j % per)) for j in range(W // 8)]

    def pack(d, carry):
        hp[d, 0:W, :] = hv[pl.ds(pl.multiple_of(d * W, 8), W), 0:128]
        packed = {}
        for j, (row, start) in enumerate(places):
            part = hv[pl.ds(pl.multiple_of(d * W + 8 * j, 8), 8), 128:256]
            if start:
                part = pltpu.roll(part, start, 1)
            packed[row] = jnp.where((lane >= start) & (lane < start + T2), part, packed.get(row, jnp.zeros((8, 128), F32)))
        for row, value in packed.items():
            hp[d, row : row + 8, :] = value
        return carry

    lax.fori_loop(0, 16, pack, 0)
    for q in range(1, 16):
        to = (dp + q) % 16
        send(hp.at[to], hv_got.at[16 - q], hs.at[q], hr.at[16 - q], (to, tp))
    total = hp[dp]
    for q in range(1, 16):
        arrived(hv_got.at[q], hr.at[q])
        total = total + hv_got[q]
    out_i[...] = total[0:W, 0:W]
    out_t[:, 0:T1] = pltpu.roll(total[0:W], T1, 1)[:, 0:T1]
    for j, (row, start) in enumerate(places):
        part = total[row : row + 8]
        if start:
            part = pltpu.roll(part, 128 - start, 1)
        out_t[8 * j : 8 * j + 8, T1:W] = part[:, 0:T2]
    for copy in started:
        copy.wait_send()


def solution(mesh):
    nz = mesh.shape["dp"] // 2
    nx = mesh.shape["tensor"] // 4

    def local(enc_i, enc_t, w_i, w_t, dw_i, dw_t, sharpness, offset):
        rows, D = enc_i.shape
        W = w_i.shape[1]
        share = rows // 16
        DX, DE = D + 128, 2 * D + 128
        scalars = jnp.concatenate([sharpness, offset])
        vmem = pl.BlockSpec(memory_space=pltpu.VMEM)
        sem = lambda n: pltpu.SemaphoreType.DMA((n,))
        return pl.pallas_call(
            functools.partial(kernel, nz, nx, D, W),
            out_shape=[jax.ShapeDtypeStruct((W, W), F32)] * 2,
            in_specs=[vmem] * 6 + [pl.BlockSpec(memory_space=pltpu.SMEM)],
            out_specs=[vmem] * 2,
            scratch_shapes=[
                pltpu.VMEM((640, D), BF16),
                pltpu.VMEM((rows, 384), BF16),
                pltpu.VMEM((16, share, 384), BF16),
                pltpu.VMEM((4, share, D), F32),
                pltpu.VMEM((32 * share, DE), BF16),
                pltpu.VMEM((8 * share, DE), BF16),
                pltpu.VMEM((32 * share, DX), F32),
                pltpu.VMEM((32 * share, 4 * share), BF16),
                pltpu.VMEM((32 * share, 4 * share), BF16),
                pltpu.VMEM((8, 4 * share), F32),
                pltpu.VMEM((32 * share, DX), BF16),
                pltpu.VMEM((8 * share, DX), BF16),
                pltpu.VMEM((16 * share, DX), BF16),
                pltpu.VMEM((16, share, DX), BF16),
                pltpu.VMEM((8, share, DX), BF16),
                pltpu.VMEM((16, share, 384), BF16),
                pltpu.VMEM((share, 384), F32),
                pltpu.VMEM((rows, 384), BF16),
                pltpu.VMEM((D, 256), F32),
                pltpu.VMEM((16, W + 16, 128), F32),
                pltpu.VMEM((16, W + 16, 128), F32),
                pltpu.VMEM((D, rows), BF16),
                pltpu.VMEM((D, rows), BF16),
            ]
            + [sem(n) for n in (16, 16, 64, 64, 8, 8, 4, 4, 16, 16, 8, 8, 16, 16, 16, 16)],
            compiler_params=pltpu.CompilerParams(
                collective_id=0, has_side_effects=True, vmem_limit_bytes=60 * 2**20
            ),
        )(enc_i, enc_t, w_i.T, w_t.T, dw_i.T, dw_t.T, scalars)

    in_specs = (
        P("dp", None),
        P("dp", None),
        P(None, "tensor"),
        P(None, "tensor"),
        P(None, "tensor"),
        P(None, "tensor"),
        P(),
        P(),
    )
    out_specs = (P("dp", "tensor"), P("dp", "tensor"))
    return jax.shard_map(local, mesh=mesh, in_specs=in_specs, out_specs=out_specs, check_vma=False)
```

```python
import functools

import jax
import jax.numpy as jnp
from jax import lax
from jax.experimental import pallas as pl
from jax.experimental.pallas import tpu as pltpu
from jax.sharding import PartitionSpec as P

EPS = 1e-06
MESH = pl.DeviceIdType.MESH
F32 = jnp.float32
BF16 = jnp.bfloat16

Z_SLOTS = (0, 3, -3, 4, 1, -1, 2, -2)
AWAY = (1, -1, 2)
XY_SLOTS = tuple(
    sorted(((i, j) for i in (0, 1, -1, 2) for j in (0, 1, -1, 2)), key=lambda p: abs(p[0]) + abs(p[1]))
)


def mirrored(back, period):
    return back if 2 * abs(back) == period else -back


def dot_nn(a, b):
    return lax.dot_general(a, b, (((1,), (0,)), ((), ())), preferred_element_type=F32)


def dot_nt(a, b):
    return lax.dot_general(a, b, (((1,), (1,)), ((), ())), preferred_element_type=F32)


def dot_tn(a, b):
    return lax.dot_general(a, b, (((0,), (0,)), ((), ())), preferred_element_type=F32)


def split_hi(value):
    hi = value.astype(BF16)
    lo = (value - hi.astype(F32)).astype(BF16)
    return hi, lo


def encoded(ends):
    lane = lax.broadcasted_iota(jnp.int32, ends.shape, 1)
    hi = ends.astype(BF16).astype(F32)
    lo = pltpu.roll(ends - hi, 2, 1)
    return jnp.where(lane < 2, hi, jnp.where(lane < 4, lo, 0.0)).astype(BF16)


def decoded(ends):
    ends = ends.astype(F32)
    return ends + pltpu.roll(ends, 126, 1)


def lanes_of(values, rows):
    lane = lax.broadcasted_iota(jnp.int32, (rows, 128), 1)
    out = jnp.zeros((rows, 128), F32)
    for index, value in enumerate(values):
        out = jnp.where(lane == index, value.astype(F32), out)
    return out


def kernel(
    nz, nx, D, W,
    enc_i, enc_t, w_i, w_t, dw_i, dw_t, sharpness, offset,
    out_i, out_t,
    wpad, x_buf, x_got, raw, img, txt, gi, pb_buf, at_buf, csum,
    si_buf, st_buf, sib_got, first_got, next_buf, next_got, rt_buf, stage, tmp, cols, hv, hp, hv_got, ent_i, ent_t,
    fs, fr, ais, air, ats, atr, gs, gr, ris, rir, rts, rtr, bs, br, hs, hr,
):
    dp = lax.axis_index("dp")
    tp = lax.axis_index("tensor")
    z, h = dp // 2, dp % 2
    y, x, c = h * 2 + tp // (2 * nx), (tp // 2) % nx, tp % 2
    rows = enc_i.shape[0]
    share = rows // 16
    half = 16 * share
    DX = D + 128
    DE = 2 * D + 128
    T0 = 80
    T1 = 128 - T0
    T2 = W - T1
    s = sharpness[0]
    bias = offset[0]

    def device_at(dz, dy, dx, core):
        zz, yy, xx = (z - dz + nz) % nz, (y - dy + 4) % 4, (x - dx + nx) % nx
        return (zz * 2 + yy // 2, ((yy % 2) * nx + xx) * 2 + core)

    tp_ids = [(tp + q) % 16 for q in range(16)]
    z_ids = [device_at(b, 0, 0, c) for b in Z_SLOTS]
    xy_ids = [device_at(0, dy, dx, c) for dx, dy in XY_SLOTS]
    z_back = [Z_SLOTS.index(mirrored(b, nz)) for b in Z_SLOTS]
    xy_back = [XY_SLOTS.index((mirrored(dx, nx), mirrored(dy, 4))) for dx, dy in XY_SLOTS]

    started = []

    def send(src, dst, ssem, rsem, device):
        copy = pltpu.make_async_remote_copy(
            src_ref=src, dst_ref=dst, send_sem=ssem, recv_sem=rsem,
            device_id=device, device_id_type=MESH,
        )
        copy.start()
        started.append(copy)

    def arrived(dst, rsem):
        pltpu.make_async_remote_copy(
            src_ref=dst, dst_ref=dst, send_sem=fs.at[0], recv_sem=rsem,
            device_id=(dp, tp), device_id_type=MESH,
        ).wait_recv()

    barrier = pltpu.get_barrier_semaphore()
    peers = [(dp, tp_ids[q]) for q in range(1, 16)]
    peers += [(z * 2 + 1 - h, (tp + 2 * q) % 16) for q in range(8)]
    peers += [((dp + q) % 16, tp) for q in range(2, 15)]
    peers += [((dp + 15 - 14 * h) % 16, tp)]
    for peer in peers:
        pl.semaphore_signal(barrier, inc=1, device_id=peer, device_id_type=MESH)

    wpad[...] = jnp.zeros_like(wpad)
    wpad[0:W] = w_i[...]
    wpad[128 : 128 + W] = dw_i[...]
    wpad[256 + T0 : 384] = w_t[0:T1]
    wpad[384 + T0 : 512] = dw_t[0:T1]
    wpad[512 : 512 + T2] = w_t[T1:W]
    wpad[544 : 544 + T2] = dw_t[T1:W]

    def project(r, carry):
        at = pl.ds(pl.multiple_of(r * 256, 256), 256)
        text = enc_t[at, :]
        x_buf[at, 0:256] = (dot_nt(enc_i[at, :], wpad[0:256]) + dot_nt(text, wpad[256:512])).astype(BF16)
        x_buf[at, 256:384] = dot_nt(text, wpad[512:640]).astype(BF16)
        return carry

    lax.fori_loop(0, rows // 256, project, 0)
    pl.semaphore_wait(barrier, len(peers))

    def share_at(index):
        return pl.ds(pl.multiple_of(index * share, share), share)

    for q in range(1, 16):
        send(x_buf.at[share_at(tp_ids[q]), :], x_got.at[tp], fs.at[q], fr.at[tp], (dp, tp_ids[q]))
    x_got[pl.ds(tp, 1)] = x_buf[share_at(tp), :].reshape(1, share, 384)
    for q in range(1, 16):
        arrived(x_got.at[tp_ids[q]], fr.at[tp_ids[q]])
    for q in range(16):
        last = x_got[q, :, 256:384].astype(F32)
        for k in range(2):
            tile = x_got[q, :, k * 128 : k * 128 + 128].astype(F32)
            raw[k, :, q * W : (q + 1) * W] = tile[:, 0:W]
            raw[2 + k, :, q * W : q * W + T1] = pltpu.roll(tile, T1, 1)[:, 0:T1]
            rest = last if k == 0 else pltpu.roll(last, 96, 1)
            raw[2 + k, :, q * W + T1 : (q + 1) * W] = rest[:, 0:T2]

    def unit_parts(values, tangent):
        radius = jnp.sqrt(jnp.sum(values * values, axis=1, keepdims=True) + EPS)
        unit = values / radius
        rate = jnp.sum(unit * tangent, axis=1, keepdims=True)
        unit_tangent = (tangent - unit * rate) / radius
        return unit, unit_tangent, radius, rate / radius

    for k, buf in ((0, img), (2, txt)):
        unit, tangent, radius, ratio = unit_parts(raw[k], raw[k + 1])
        buf[0:share, 0:D] = unit.astype(BF16)
        buf[0:share, D : 2 * D] = tangent.astype(BF16)
        hi, lo = split_hi(ratio)
        buf[0:share, 2 * D : DE] = lanes_of((hi, lo), share).astype(BF16)

    parts = ((0, D), (D, DE - D))
    counts = {"i": 0, "t": 0}
    sib = (dp, tp + 1 - 2 * c)

    def ipart(slot, part):
        return img.at[pl.ds(slot * share, share), pl.ds(*parts[part])]

    def tat(slot):
        return txt.at[pl.ds(slot * share, share), :]

    def isend(src, dst, part, device):
        send(ipart(src, part), ipart(dst, part), ais.at[counts["i"]], air.at[part * 32 + dst], device)
        counts["i"] += 1

    def hop(pos, axis, way, part):
        to = list(pos)
        to[axis] = 2 if abs(pos[axis] + way) == 2 else pos[axis] + way
        away = [0, 0]
        away[axis] = -way
        isend(XY_SLOTS.index(pos), XY_SLOTS.index(tuple(to)), part, device_at(0, away[1], away[0], c))

    def i_on(pos, part):
        first, second = (0, 1) if part == 0 else (1, 0)
        if pos[second] == 0:
            if pos[first] >= 0 and (pos[first] == 0 or (part == 0 and pos[first] == 1)):
                hop(pos, first, 1, part)
            if pos[first] == 0 or (part == 1 and pos[first] == -1):
                hop(pos, first, -1, part)
            hop(pos, second, 1, part)
            hop(pos, second, -1, part)
        else:
            forth = pos[first] in (0, 2)
            if pos[second] == 1 and forth:
                hop(pos, second, 1, part)
            if pos[second] == -1 and not forth:
                hop(pos, second, -1, part)
        isend(XY_SLOTS.index(pos), 16 + XY_SLOTS.index(pos), part, sib)

    def i_step(pos):
        for part in (0, 1):
            slot = XY_SLOTS.index(pos)
            arrived(ipart(slot, part), air.at[part * 32 + slot])
            i_on(pos, part)

    def tsend(src, dst, device):
        send(tat(src), tat(dst), ats.at[counts["t"]], atr.at[dst], device)
        counts["t"] += 1

    def t_on(back):
        src = Z_SLOTS.index(back)
        if 0 <= back < 3:
            tsend(src, Z_SLOTS.index(back + 1), device_at(-1, 0, 0, c))
        if -3 < back <= 0:
            tsend(src, Z_SLOTS.index(back - 1), device_at(1, 0, 0, c))

    def twait(back):
        slot = Z_SLOTS.index(back)
        arrived(tat(slot), atr.at[slot])

    for part in (0, 1):
        i_on((0, 0), part)
    t_on(0)
    for k in range(D // 128):
        ka = pl.ds(k * 128, 128)
        ent_i[ka, :] = enc_i[:, ka].T
        ent_t[ka, :] = enc_t[:, ka].T
    eye = lanes_of([(lax.broadcasted_iota(jnp.int32, (8, 1), 0) == k) for k in range(8)], 8).astype(BF16)
    first_two = jnp.where(lax.broadcasted_iota(jnp.int32, (8, 128), 1) < 2, 1.0, 0.0).astype(BF16)
    TC = 4 * share
    RB = 8 * share

    def prepare(ci):
        csum[...] = jnp.zeros_like(csum)
        return dot_nt(first_two, txt[ci * TC : (ci + 1) * TC, 2 * D : DE])[0:1, :]

    def blocks(ci, sigma, low, high):
        at = pl.ds(ci * TC, TC)

        def block(r, carry):
            ra = pl.ds(pl.multiple_of(r * RB, RB), RB)
            tu = txt[at, 0:D]
            tt = txt[at, D : 2 * D]
            iu = img[ra, 0:D]
            it = img[ra, D : 2 * D]
            extra = img[ra, 2 * D : DE].astype(F32)
            rho = extra[:, 0:1] + extra[:, 1:2]
            cosine = dot_nt(iu, tu)
            cross = dot_nt(it, tu) + dot_nt(iu, tt)
            prob = jax.nn.sigmoid(s * cosine + bias)
            rate = prob * (1.0 - prob) * (s * cross)
            pb = prob.astype(BF16)
            q1 = prob * cosine
            q2 = prob * cross + rate * cosine
            csum[0:1, :] += jnp.sum(q1, axis=0, keepdims=True)
            csum[1:2, :] += jnp.sum(q2, axis=0, keepdims=True)
            pb_buf[ra, :] = pb
            at_buf[ra, :] = (rate - sigma * prob).astype(BF16)
            gain = dot_nn((rate - rho * prob).astype(BF16), tu) + dot_nn(pb, tt)
            sums = lanes_of((jnp.sum(q1, axis=1, keepdims=True), jnp.sum(q2, axis=1, keepdims=True)), RB)
            if ci == 0:
                gi[ra, 0:D] = gain
                gi[ra, D:DX] = sums
            else:
                gi[ra, 0:D] += gain
                gi[ra, D:DX] += sums
            return carry

        lax.fori_loop(low, high, block, 0)

    def text_sums(ci):
        at = pl.ds(ci * TC, TC)
        hi, lo = split_hi(csum[...])
        tops = jnp.concatenate([hi[0:2].astype(F32), lo[0:2].astype(F32), jnp.zeros((4, TC), F32)], axis=0)
        st_buf[at, D:DX] = dot_tn(tops.astype(BF16), eye).astype(BF16)
        for k in range(0, D, 256):
            e = min(k + 256, D)
            gain = dot_tn(at_buf[...], img[:, k:e]) + dot_tn(pb_buf[...], img[:, D + k : D + e])
            st_buf[at, k:e] = gain.astype(BF16)
        for q in range(4 * ci, 4 * ci + 4):
            if q > 0:
                k = z_back[q]
                send(st_buf.at[pl.ds(q * share, share), :], rt_buf.at[k], rts.at[q], rtr.at[k], z_ids[q])

    def sums_out(row):
        at = pl.ds(row, share)
        si_buf[at, 0:D] = gi[at, 0:D].astype(BF16)
        si_buf[at, D:DX] = encoded(gi[at, D:DX])

    H = DX // 2
    halves = (pl.ds(0, H), pl.ds(H, H))
    counts["r"] = 0

    def rsend(src, dst, at, device):
        send(src, dst, ris.at[counts["r"]], rir.at[at], device)
        counts["r"] += 1

    def add_in(row, part, got):
        at = pl.ds(row, share)
        if part == 0:
            gi[at, 0:H] += got.astype(F32)
        else:
            gi[at, H:D] += got[:, 0 : D - H].astype(F32)
            gi[at, D:DX] += decoded(got[:, D - H : H])

    def to_sibling():
        for g in range(4):
            def one(q, carry):
                sums_out(pl.multiple_of(half + (4 * g + q) * share, share))
                return carry
            lax.fori_loop(0, 4, one, 0)
            src = si_buf.at[pl.ds(half + 4 * g * share, 4 * share), :]
            send(src, sib_got.at[pl.ds(4 * g * share, 4 * share), :], gs.at[g], gr.at[g], sib)

    for pos in XY_SLOTS[1:5]:
        i_step(pos)
    for back in (1, -1):
        twait(back)
        t_on(back)
    for pos in XY_SLOTS[5:8]:
        i_step(pos)
    for back in (2, -2):
        twait(back)
        t_on(back)
    for pos in XY_SLOTS[8:11]:
        i_step(pos)
    for back in (3, -3):
        twait(back)
    far = Z_SLOTS.index(3) + c * (Z_SLOTS.index(-3) - Z_SLOTS.index(3))
    tsend(far, Z_SLOTS.index(4), device_at(2 * c - 1, 0, 0, c))
    for pos in XY_SLOTS[11:15]:
        i_step(pos)
    twait(4)
    sigma = prepare(0)
    blocks(0, sigma, 0, 1)
    for pos in XY_SLOTS[15:16]:
        i_step(pos)
    blocks(0, sigma, 1, 2)
    for slot in range(16):
        for part in (0, 1):
            arrived(ipart(16 + slot, part), air.at[part * 32 + 16 + slot])
    blocks(0, sigma, 2, 4)
    text_sums(0)
    sigma = prepare(1)
    blocks(1, sigma, 2, 4)
    to_sibling()
    blocks(1, sigma, 0, 2)

    near = (0,) + AWAY
    for g in range(4):
        arrived(sib_got.at[pl.ds(4 * g * share, 4 * share), :], gr.at[g])
        for q in range(4 * g, 4 * g + 4):
            qa = pl.ds(q * share, share)
            gi[qa, 0:D] += sib_got[qa, 0:D].astype(F32)
            gi[qa, D:DX] += decoded(sib_got[qa, D:DX])
            if q == 0:
                continue
            sums_out(q * share)
            dx, dy = XY_SLOTS[q]
            for part, off, keep in ((0, dy, dx), (1, dx, dy)):
                if off:
                    at = part * 12 + AWAY.index(mirrored(off, 4)) * 4 + near.index(keep)
                    to = device_at(0, dy, 0, c) if part == 0 else device_at(0, 0, dx, c)
                    rsend(si_buf.at[qa, halves[part]], first_got.at[at], at, to)
    text_sums(1)
    for keep in AWAY + (0,):
        for part in (0, 1):
            row = XY_SLOTS.index((keep, 0) if part == 0 else (0, keep)) * share
            for o in range(3):
                at = part * 12 + o * 4 + near.index(keep)
                arrived(first_got.at[at], rir.at[at])
                add_in(row, part, first_got[at])
            if keep == 0:
                continue
            at = part * 3 + AWAY.index(keep)
            ra = pl.ds(row, share)
            if part == 0:
                next_buf[at] = gi[ra, 0:H].astype(BF16)
                to = device_at(0, 0, keep, c)
            else:
                next_buf[at, :, 0 : D - H] = gi[ra, H:D].astype(BF16)
                next_buf[at, :, D - H : H] = encoded(gi[ra, D:DX])
                to = device_at(0, keep, 0, c)
            k = part * 3 + AWAY.index(mirrored(keep, 4))
            rsend(next_buf.at[at], next_got.at[k], 24 + k, to)

    for q in range(1, 8):
        arrived(rt_buf.at[q], rtr.at[q])
    for q in range(6):
        arrived(next_got.at[q], rir.at[24 + q])
        add_in(0, q // 3, next_got[q])

    iu, it = img[0:share, 0:D].astype(F32), img[0:share, D : 2 * D].astype(F32)
    tu, tt = txt[0:share, 0:D].astype(F32), txt[0:share, D : 2 * D].astype(F32)
    pair_cos = jnp.sum(iu * tu, axis=1, keepdims=True)
    pair_cross = jnp.sum(it * tu + iu * tt, axis=1, keepdims=True)
    tmp[...] = jnp.zeros_like(tmp)
    for k in range(2):
        if k == 0:
            total = gi[0:share, 0:D]
            inner = gi[0:share, D : D + 1]
            inner_rate = gi[0:share, D + 1 : D + 2]
            more = []
            other, other_tangent = tu, tt
        else:
            total, inner, inner_rate = 0.0, 0.0, 0.0
            more = [st_buf[0:share, :]] + [rt_buf[q] for q in range(1, 8)]
            other, other_tangent = iu, it
        for term in more:
            total = total + term[:, 0:D].astype(F32)
            ends = term[:, D:DX].astype(F32)
            inner = inner + (ends[:, 0:1] + ends[:, 2:3])
            inner_rate = inner_rate + (ends[:, 1:2] + ends[:, 3:4])
        unit, tangent, radius, ratio = unit_parts(raw[2 * k], raw[2 * k + 1])
        total = s * (total + (ratio * other - other_tangent))
        inner = s * (inner - pair_cos)
        inner_rate = s * (inner_rate - pair_cross)
        back = (total - tangent * inner - unit * (inner_rate - ratio * inner)) / radius
        hi, lo = split_hi(back)
        raw[2 * k] = hi.astype(F32)
        raw[2 * k + 1] = lo.astype(F32)
    for q in range(16):
        for k in range(2):
            tmp[:, k * 128 : k * 128 + W] = raw[k, :, q * W : (q + 1) * W]
            tmp[:, k * 128 + T0 : k * 128 + 128] = raw[2 + k, :, q * W : q * W + T1]
            tmp[:, 256 + 32 * k : 256 + 32 * k + T2] = raw[2 + k, :, q * W + T1 : (q + 1) * W]
        stage[q] = tmp[...].astype(BF16)

    for q in range(1, 16):
        send(stage.at[tp_ids[q]], cols.at[share_at(tp), :], bs.at[q], br.at[tp], (dp, tp_ids[q]))
    cols[share_at(tp), :] = stage[pl.ds(tp, 1)].reshape(share, 384)
    for q in range(1, 16):
        arrived(cols.at[share_at(tp_ids[q]), :], br.at[tp_ids[q]])

    lane = lax.broadcasted_iota(jnp.int32, (8, 128), 1)
    text_lane = lax.broadcasted_iota(jnp.int32, (128, 128), 1) >= T0

    def head(k, carry):
        ka = pl.ds(pl.multiple_of(k * 128, 128), 128)
        of_i = dot_nn(ent_i[ka, :], cols[:, 0:256])
        of_t = dot_nn(ent_t[ka, :], cols[...])
        hv[ka, 0:128] = jnp.where(text_lane, of_t[:, 0:128] + of_t[:, 128:256], of_i[:, 0:128] + of_i[:, 128:256])
        rest = of_t[:, 256:384]
        hv[ka, 128:256] = rest + pltpu.roll(rest, 96, 1)
        return carry

    lax.fori_loop(0, D // 128, head, 0)

    per = 128 // T2
    places = [(W + 8 * (j // per), T2 * (j % per)) for j in range(W // 8)]

    def pack(d, carry):
        hp[d, 0:W, :] = hv[pl.ds(pl.multiple_of(d * W, 8), W), 0:128]
        packed = {}
        for j, (row, start) in enumerate(places):
            part = hv[pl.ds(pl.multiple_of(d * W + 8 * j, 8), 8), 128:256]
            if start:
                part = pltpu.roll(part, start, 1)
            packed[row] = jnp.where((lane >= start) & (lane < start + T2), part, packed.get(row, jnp.zeros((8, 128), F32)))
        for row, value in packed.items():
            hp[d, row : row + 8, :] = value
        return carry

    lax.fori_loop(0, 16, pack, 0)
    for q in range(1, 16):
        to = (dp + q) % 16
        send(hp.at[to], hv_got.at[16 - q], hs.at[q], hr.at[16 - q], (to, tp))
    total = hp[dp]
    for q in range(1, 16):
        arrived(hv_got.at[q], hr.at[q])
        total = total + hv_got[q]
    out_i[...] = total[0:W, 0:W]
    out_t[:, 0:T1] = pltpu.roll(total[0:W], T1, 1)[:, 0:T1]
    for j, (row, start) in enumerate(places):
        part = total[row : row + 8]
        if start:
            part = pltpu.roll(part, 128 - start, 1)
        out_t[8 * j : 8 * j + 8, T1:W] = part[:, 0:T2]
    for copy in started:
        copy.wait_send()


def solution(mesh):
    nz = mesh.shape["dp"] // 2
    nx = mesh.shape["tensor"] // 4

    def local(enc_i, enc_t, w_i, w_t, dw_i, dw_t, sharpness, offset):
        rows, D = enc_i.shape
        W = w_i.shape[1]
        share = rows // 16
        DX, DE = D + 128, 2 * D + 128
        vmem = pl.BlockSpec(memory_space=pltpu.VMEM)
        sem = lambda n: pltpu.SemaphoreType.DMA((n,))
        return pl.pallas_call(
            functools.partial(kernel, nz, nx, D, W),
            out_shape=[jax.ShapeDtypeStruct((W, W), F32)] * 2,
            in_specs=[vmem] * 6 + [pl.BlockSpec(memory_space=pltpu.SMEM)] * 2,
            out_specs=[vmem] * 2,
            scratch_shapes=[
                pltpu.VMEM((640, D), BF16),
                pltpu.VMEM((rows, 384), BF16),
                pltpu.VMEM((16, share, 384), BF16),
                pltpu.VMEM((4, share, D), F32),
                pltpu.VMEM((32 * share, DE), BF16),
                pltpu.VMEM((8 * share, DE), BF16),
                pltpu.VMEM((32 * share, DX), F32),
                pltpu.VMEM((32 * share, 4 * share), BF16),
                pltpu.VMEM((32 * share, 4 * share), BF16),
                pltpu.VMEM((8, 4 * share), F32),
                pltpu.VMEM((32 * share, DX), BF16),
                pltpu.VMEM((8 * share, DX), BF16),
                pltpu.VMEM((16 * share, DX), BF16),
                pltpu.VMEM((24, share, DX // 2), BF16),
                pltpu.VMEM((6, share, DX // 2), BF16),
                pltpu.VMEM((6, share, DX // 2), BF16),
                pltpu.VMEM((8, share, DX), BF16),
                pltpu.VMEM((16, share, 384), BF16),
                pltpu.VMEM((share, 384), F32),
                pltpu.VMEM((rows, 384), BF16),
                pltpu.VMEM((D, 256), F32),
                pltpu.VMEM((16, W + 16, 128), F32),
                pltpu.VMEM((16, W + 16, 128), F32),
                pltpu.VMEM((D, rows), BF16),
                pltpu.VMEM((D, rows), BF16),
            ]
            + [sem(n) for n in (16, 16, 64, 64, 8, 8, 4, 4, 32, 32, 8, 8, 16, 16, 16, 16)],
            compiler_params=pltpu.CompilerParams(
                collective_id=0, has_side_effects=True, vmem_limit_bytes=60 * 2**20
            ),
        )(enc_i, enc_t, w_i.T, w_t.T, dw_i.T, dw_t.T, sharpness, offset)

    in_specs = (
        P("dp", None),
        P("dp", None),
        P(None, "tensor"),
        P(None, "tensor"),
        P(None, "tensor"),
        P(None, "tensor"),
        P(),
        P(),
    )
    out_specs = (P("dp", "tensor"), P("dp", "tensor"))
    return jax.shard_map(local, mesh=mesh, in_specs=in_specs, out_specs=out_specs, check_vma=False)
```

```python
import functools

import jax
import jax.numpy as jnp
from jax import lax
from jax.experimental import pallas as pl
from jax.experimental.pallas import tpu as pltpu
from jax.sharding import PartitionSpec as P

EPS = 1e-06
MESH = pl.DeviceIdType.MESH
F32 = jnp.float32
BF16 = jnp.bfloat16

Z_SLOTS = (0, 3, -3, 4, 1, -1, 2, -2)
AWAY = (1, -1, 2)
XY_SLOTS = tuple(
    sorted(((i, j) for i in (0, 1, -1, 2) for j in (0, 1, -1, 2)), key=lambda p: abs(p[0]) + abs(p[1]))
)


def mirrored(back, period):
    return back if 2 * abs(back) == period else -back


def dot_nn(a, b):
    return lax.dot_general(a, b, (((1,), (0,)), ((), ())), preferred_element_type=F32)


def dot_nt(a, b):
    return lax.dot_general(a, b, (((1,), (1,)), ((), ())), preferred_element_type=F32)


def dot_tn(a, b):
    return lax.dot_general(a, b, (((0,), (0,)), ((), ())), preferred_element_type=F32)


def split_hi(value):
    hi = value.astype(BF16)
    lo = (value - hi.astype(F32)).astype(BF16)
    return hi, lo


def encoded(ends):
    lane = lax.broadcasted_iota(jnp.int32, ends.shape, 1)
    hi = ends.astype(BF16).astype(F32)
    lo = pltpu.roll(ends - hi, 2, 1)
    return jnp.where(lane < 2, hi, jnp.where(lane < 4, lo, 0.0)).astype(BF16)


def decoded(ends):
    ends = ends.astype(F32)
    return ends + pltpu.roll(ends, 126, 1)


def lanes_of(values, rows):
    lane = lax.broadcasted_iota(jnp.int32, (rows, 128), 1)
    out = jnp.zeros((rows, 128), F32)
    for index, value in enumerate(values):
        out = jnp.where(lane == index, value.astype(F32), out)
    return out


def kernel(
    nz, nx, D, W,
    from_i, from_t, w_i, w_t, dw_i, dw_t, sharpness, offset,
    out_i, out_t,
    enc_i, enc_t, cs, wpad, x_buf, x_got, raw, img, txt, gi, pb_buf, at_buf, csum,
    si_buf, st_buf, sib_got, first_got, next_buf, next_got, rt_buf, stage, tmp, cols, hv, hp, hv_got, ent_i, ent_t,
    fs, fr, ais, air, ats, atr, gs, gr, ris, rir, rts, rtr, bs, br, hs, hr,
):
    dp = lax.axis_index("dp")
    tp = lax.axis_index("tensor")
    z, h = dp // 2, dp % 2
    y, x, c = h * 2 + tp // (2 * nx), (tp // 2) % nx, tp % 2
    rows = enc_i.shape[0]
    share = rows // 16
    half = 16 * share
    DX = D + 128
    DE = 2 * D + 128
    T0 = 80
    T1 = 128 - T0
    T2 = W - T1
    s = sharpness[0]
    bias = offset[0]

    def device_at(dz, dy, dx, core):
        zz, yy, xx = (z - dz + nz) % nz, (y - dy + 4) % 4, (x - dx + nx) % nx
        return (zz * 2 + yy // 2, ((yy % 2) * nx + xx) * 2 + core)

    tp_ids = [(tp + q) % 16 for q in range(16)]
    z_ids = [device_at(b, 0, 0, c) for b in Z_SLOTS]
    xy_ids = [device_at(0, dy, dx, c) for dx, dy in XY_SLOTS]
    z_back = [Z_SLOTS.index(mirrored(b, nz)) for b in Z_SLOTS]
    xy_back = [XY_SLOTS.index((mirrored(dx, nx), mirrored(dy, 4))) for dx, dy in XY_SLOTS]

    started = []

    def send(src, dst, ssem, rsem, device):
        copy = pltpu.make_async_remote_copy(
            src_ref=src, dst_ref=dst, send_sem=ssem, recv_sem=rsem,
            device_id=device, device_id_type=MESH,
        )
        copy.start()
        started.append(copy)

    def arrived(dst, rsem):
        pltpu.make_async_remote_copy(
            src_ref=dst, dst_ref=dst, send_sem=fs.at[0], recv_sem=rsem,
            device_id=(dp, tp), device_id_type=MESH,
        ).wait_recv()

    loads = [pltpu.make_async_copy(a, b, cs.at[k]) for k, (a, b) in enumerate(((from_i, enc_i), (from_t, enc_t)))]
    for load in loads:
        load.start()

    barrier = pltpu.get_barrier_semaphore()
    peers = [(dp, tp_ids[q]) for q in range(1, 16)]
    peers += [(z * 2 + 1 - h, (tp + 2 * q) % 16) for q in range(8)]
    peers += [((dp + q) % 16, tp) for q in range(2, 15)]
    peers += [((dp + 15 - 14 * h) % 16, tp)]
    for peer in peers:
        pl.semaphore_signal(barrier, inc=1, device_id=peer, device_id_type=MESH)

    wpad[...] = jnp.zeros_like(wpad)
    wpad[0:W] = w_i[...]
    wpad[128 : 128 + W] = dw_i[...]
    wpad[256 + T0 : 384] = w_t[0:T1]
    wpad[384 + T0 : 512] = dw_t[0:T1]
    wpad[512 : 512 + T2] = w_t[T1:W]
    wpad[544 : 544 + T2] = dw_t[T1:W]

    def share_at(index):
        return pl.ds(pl.multiple_of(index * share, share), share)

    for load in loads:
        load.wait()

    for step in range(2):
        side = tp // 8 if step == 0 else 1 - tp // 8

        def project(r, carry):
            at = pl.ds(pl.multiple_of(side * (rows // 2) + r * (rows // 4), rows // 4), rows // 4)
            text = enc_t[at, :]
            x_buf[at, 0:256] = (dot_nt(enc_i[at, :], wpad[0:256]) + dot_nt(text, wpad[256:512])).astype(BF16)
            x_buf[at, 256:384] = dot_nt(text, wpad[512:640]).astype(BF16)
            return carry

        lax.fori_loop(0, 2, project, 0)
        if step == 0:
            pl.semaphore_wait(barrier, len(peers))
        for q in range(1 - step, 8):
            to = side * 8 + (tp + q) % 8
            send(x_buf.at[share_at(to), :], x_got.at[tp], fs.at[step * 8 + q], fr.at[tp], (dp, to))
    x_got[pl.ds(tp, 1)] = x_buf[share_at(tp), :].reshape(1, share, 384)
    for q in range(1, 16):
        arrived(x_got.at[tp_ids[q]], fr.at[tp_ids[q]])
    for q in range(16):
        last = x_got[q, :, 256:384].astype(F32)
        for k in range(2):
            tile = x_got[q, :, k * 128 : k * 128 + 128].astype(F32)
            raw[k, :, q * W : (q + 1) * W] = tile[:, 0:W]
            raw[2 + k, :, q * W : q * W + T1] = pltpu.roll(tile, T1, 1)[:, 0:T1]
            rest = last if k == 0 else pltpu.roll(last, 96, 1)
            raw[2 + k, :, q * W + T1 : (q + 1) * W] = rest[:, 0:T2]

    def unit_parts(values, tangent):
        radius = jnp.sqrt(jnp.sum(values * values, axis=1, keepdims=True) + EPS)
        inverse = 1.0 / radius
        unit = values * inverse
        rate = jnp.sum(unit * tangent, axis=1, keepdims=True)
        unit_tangent = (tangent - unit * rate) * inverse
        return unit, unit_tangent, inverse, rate * inverse

    for k, buf in ((0, img), (2, txt)):
        unit, tangent, inverse, ratio = unit_parts(raw[k], raw[k + 1])
        buf[0:share, 0:D] = unit.astype(BF16)
        buf[0:share, D : 2 * D] = tangent.astype(BF16)
        hi, lo = split_hi(ratio)
        buf[0:share, 2 * D : DE] = lanes_of((hi, lo), share).astype(BF16)

    parts = ((0, D), (D, DE - D))
    counts = {"i": 0, "t": 0}
    sib = (dp, tp + 1 - 2 * c)

    def ipart(slot, part):
        return img.at[pl.ds(slot * share, share), pl.ds(*parts[part])]

    def tat(slot):
        return txt.at[pl.ds(slot * share, share), :]

    def isend(src, dst, part, device):
        send(ipart(src, part), ipart(dst, part), ais.at[counts["i"]], air.at[part * 32 + dst], device)
        counts["i"] += 1

    def hop(pos, axis, way, part):
        to = list(pos)
        to[axis] = 2 if abs(pos[axis] + way) == 2 else pos[axis] + way
        away = [0, 0]
        away[axis] = -way
        isend(XY_SLOTS.index(pos), XY_SLOTS.index(tuple(to)), part, device_at(0, away[1], away[0], c))

    def i_on(pos, part):
        first, second = (0, 1) if part == 0 else (1, 0)
        if pos[second] == 0:
            if pos[first] >= 0 and (pos[first] == 0 or (part == 0 and pos[first] == 1)):
                hop(pos, first, 1, part)
            if pos[first] == 0 or (part == 1 and pos[first] == -1):
                hop(pos, first, -1, part)
            hop(pos, second, 1, part)
            hop(pos, second, -1, part)
        else:
            forth = pos[first] in (0, 2)
            if pos[second] == 1 and forth:
                hop(pos, second, 1, part)
            if pos[second] == -1 and not forth:
                hop(pos, second, -1, part)
        isend(XY_SLOTS.index(pos), 16 + XY_SLOTS.index(pos), part, sib)

    def i_step(pos):
        for part in (0, 1):
            slot = XY_SLOTS.index(pos)
            arrived(ipart(slot, part), air.at[part * 32 + slot])
            i_on(pos, part)

    def tsend(src, dst, device):
        send(tat(src), tat(dst), ats.at[counts["t"]], atr.at[dst], device)
        counts["t"] += 1

    def t_on(back):
        src = Z_SLOTS.index(back)
        if 0 <= back < 3:
            tsend(src, Z_SLOTS.index(back + 1), device_at(-1, 0, 0, c))
        if -3 < back <= 0:
            tsend(src, Z_SLOTS.index(back - 1), device_at(1, 0, 0, c))

    def twait(back):
        slot = Z_SLOTS.index(back)
        arrived(tat(slot), atr.at[slot])

    for part in (0, 1):
        i_on((0, 0), part)
    t_on(0)
    for k in range(D // 128):
        ka = pl.ds(k * 128, 128)
        ent_i[ka, :] = enc_i[:, ka].T
        ent_t[ka, :] = enc_t[:, ka].T
    eye = lanes_of([(lax.broadcasted_iota(jnp.int32, (8, 1), 0) == k) for k in range(8)], 8).astype(BF16)
    first_two = jnp.where(lax.broadcasted_iota(jnp.int32, (8, 128), 1) < 2, 1.0, 0.0).astype(BF16)
    TC = 4 * share
    RB = 8 * share

    def prepare(ci):
        csum[...] = jnp.zeros_like(csum)
        return dot_nt(first_two, txt[ci * TC : (ci + 1) * TC, 2 * D : DE])[0:1, :]

    def blocks(ci, sigma, low, high):
        at = pl.ds(ci * TC, TC)

        def block(r, carry):
            ra = pl.ds(pl.multiple_of(r * RB, RB), RB)
            tu = txt[at, 0:D]
            tt = txt[at, D : 2 * D]
            iu = img[ra, 0:D]
            it = img[ra, D : 2 * D]
            extra = img[ra, 2 * D : DE].astype(F32)
            rho = extra[:, 0:1] + extra[:, 1:2]
            cosine = dot_nt(iu, tu)
            cross = dot_nt(it, tu) + dot_nt(iu, tt)
            prob = jax.nn.sigmoid(s * cosine + bias)
            rate = prob * (1.0 - prob) * (s * cross)
            pb = prob.astype(BF16)
            q1 = prob * cosine
            q2 = prob * cross + rate * cosine
            csum[0:1, :] += jnp.sum(q1, axis=0, keepdims=True)
            csum[1:2, :] += jnp.sum(q2, axis=0, keepdims=True)
            pb_buf[ra, :] = pb
            at_buf[ra, :] = (rate - sigma * prob).astype(BF16)
            gain = dot_nn((rate - rho * prob).astype(BF16), tu) + dot_nn(pb, tt)
            sums = lanes_of((jnp.sum(q1, axis=1, keepdims=True), jnp.sum(q2, axis=1, keepdims=True)), RB)
            if ci == 0:
                gi[ra, 0:D] = gain
                gi[ra, D:DX] = sums
            else:
                gi[ra, 0:D] += gain
                gi[ra, D:DX] += sums
            return carry

        lax.fori_loop(low, high, block, 0)

    def text_sums(ci):
        at = pl.ds(ci * TC, TC)
        hi, lo = split_hi(csum[...])
        tops = jnp.concatenate([hi[0:2].astype(F32), lo[0:2].astype(F32), jnp.zeros((4, TC), F32)], axis=0)
        st_buf[at, D:DX] = dot_tn(tops.astype(BF16), eye).astype(BF16)
        for k in range(0, D, 256):
            e = min(k + 256, D)
            gain = dot_tn(at_buf[...], img[:, k:e]) + dot_tn(pb_buf[...], img[:, D + k : D + e])
            st_buf[at, k:e] = gain.astype(BF16)
        for q in range(4 * ci, 4 * ci + 4):
            if q > 0:
                k = z_back[q]
                send(st_buf.at[pl.ds(q * share, share), :], rt_buf.at[k], rts.at[q], rtr.at[k], z_ids[q])

    def sums_out(row):
        at = pl.ds(row, share)
        si_buf[at, 0:D] = gi[at, 0:D].astype(BF16)
        si_buf[at, D:DX] = encoded(gi[at, D:DX])

    H = DX // 2
    halves = (pl.ds(0, H), pl.ds(H, H))
    counts["r"] = 0

    def rsend(src, dst, at, device):
        send(src, dst, ris.at[counts["r"]], rir.at[at], device)
        counts["r"] += 1

    def add_in(row, part, got):
        at = pl.ds(row, share)
        if part == 0:
            gi[at, 0:H] += got.astype(F32)
        else:
            gi[at, H:D] += got[:, 0 : D - H].astype(F32)
            gi[at, D:DX] += decoded(got[:, D - H : H])

    def to_sibling(first, last):
        for g in range(first, last):
            def one(q, carry):
                sums_out(pl.multiple_of(half + (4 * g + q) * share, share))
                return carry
            lax.fori_loop(0, 4, one, 0)
            src = si_buf.at[pl.ds(half + 4 * g * share, 4 * share), :]
            send(src, sib_got.at[pl.ds(4 * g * share, 4 * share), :], gs.at[g], gr.at[g], sib)

    for pos in XY_SLOTS[1:5]:
        i_step(pos)
    for back in (1, -1):
        twait(back)
        t_on(back)
    for pos in XY_SLOTS[5:8]:
        i_step(pos)
    for back in (2, -2):
        twait(back)
        t_on(back)
    for pos in XY_SLOTS[8:11]:
        i_step(pos)
    for back in (3, -3):
        twait(back)
    far = Z_SLOTS.index(3) + c * (Z_SLOTS.index(-3) - Z_SLOTS.index(3))
    tsend(far, Z_SLOTS.index(4), device_at(2 * c - 1, 0, 0, c))
    for pos in XY_SLOTS[11:15]:
        i_step(pos)
    twait(4)
    sigma = prepare(0)
    blocks(0, sigma, 0, 1)
    for pos in XY_SLOTS[15:16]:
        i_step(pos)
    blocks(0, sigma, 1, 2)
    for slot in range(16):
        for part in (0, 1):
            arrived(ipart(16 + slot, part), air.at[part * 32 + 16 + slot])
    blocks(0, sigma, 2, 4)
    text_sums(0)
    sigma = prepare(1)
    blocks(1, sigma, 2, 3)
    to_sibling(0, 2)
    blocks(1, sigma, 3, 4)
    to_sibling(2, 4)

    near = (0,) + AWAY
    for g in range(4):
        if g % 2 == 0:
            blocks(1, sigma, g // 2, g // 2 + 1)
        arrived(sib_got.at[pl.ds(4 * g * share, 4 * share), :], gr.at[g])
        for q in range(4 * g, 4 * g + 4):
            qa = pl.ds(q * share, share)
            gi[qa, 0:D] += sib_got[qa, 0:D].astype(F32)
            gi[qa, D:DX] += decoded(sib_got[qa, D:DX])
            if q == 0:
                continue
            sums_out(q * share)
            dx, dy = XY_SLOTS[q]
            for part, off, keep in ((0, dy, dx), (1, dx, dy)):
                if off:
                    at = part * 12 + AWAY.index(mirrored(off, 4)) * 4 + near.index(keep)
                    to = device_at(0, dy, 0, c) if part == 0 else device_at(0, 0, dx, c)
                    rsend(si_buf.at[qa, halves[part]], first_got.at[at], at, to)
    text_sums(1)
    for keep in AWAY + (0,):
        for part in (0, 1):
            row = XY_SLOTS.index((keep, 0) if part == 0 else (0, keep)) * share
            for o in range(3):
                at = part * 12 + o * 4 + near.index(keep)
                arrived(first_got.at[at], rir.at[at])
                add_in(row, part, first_got[at])
            if keep == 0:
                continue
            at = part * 3 + AWAY.index(keep)
            ra = pl.ds(row, share)
            if part == 0:
                next_buf[at] = gi[ra, 0:H].astype(BF16)
                to = device_at(0, 0, keep, c)
            else:
                next_buf[at, :, 0 : D - H] = gi[ra, H:D].astype(BF16)
                next_buf[at, :, D - H : H] = encoded(gi[ra, D:DX])
                to = device_at(0, keep, 0, c)
            k = part * 3 + AWAY.index(mirrored(keep, 4))
            rsend(next_buf.at[at], next_got.at[k], 24 + k, to)

    for q in range(1, 8):
        arrived(rt_buf.at[q], rtr.at[q])
    iu, it = img[0:share, 0:D].astype(F32), img[0:share, D : 2 * D].astype(F32)
    tu, tt = txt[0:share, 0:D].astype(F32), txt[0:share, D : 2 * D].astype(F32)
    pair_cos = jnp.sum(iu * tu, axis=1, keepdims=True)
    pair_cross = jnp.sum(it * tu + iu * tt, axis=1, keepdims=True)
    tmp[...] = jnp.zeros_like(tmp)
    for k in (1, 0):
        if k == 0:
            for q in range(6):
                arrived(next_got.at[q], rir.at[24 + q])
                add_in(0, q // 3, next_got[q])
            total = gi[0:share, 0:D]
            inner = gi[0:share, D : D + 1]
            inner_rate = gi[0:share, D + 1 : D + 2]
            more = []
            other, other_tangent = tu, tt
        else:
            total, inner, inner_rate = 0.0, 0.0, 0.0
            more = [st_buf[0:share, :]] + [rt_buf[q] for q in range(1, 8)]
            other, other_tangent = iu, it
        for term in more:
            total = total + term[:, 0:D].astype(F32)
            ends = term[:, D:DX].astype(F32)
            inner = inner + (ends[:, 0:1] + ends[:, 2:3])
            inner_rate = inner_rate + (ends[:, 1:2] + ends[:, 3:4])
        unit, tangent, inverse, ratio = unit_parts(raw[2 * k], raw[2 * k + 1])
        total = s * (total + (ratio * other - other_tangent))
        inner = s * (inner - pair_cos)
        inner_rate = s * (inner_rate - pair_cross)
        back = (total - tangent * inner - unit * (inner_rate - ratio * inner)) * inverse
        hi, lo = split_hi(back)
        raw[2 * k] = hi.astype(F32)
        raw[2 * k + 1] = lo.astype(F32)
    for q in range(16):
        for k in range(2):
            tmp[:, k * 128 : k * 128 + W] = raw[k, :, q * W : (q + 1) * W]
            tmp[:, k * 128 + T0 : k * 128 + 128] = raw[2 + k, :, q * W : q * W + T1]
            tmp[:, 256 + 32 * k : 256 + 32 * k + T2] = raw[2 + k, :, q * W + T1 : (q + 1) * W]
        stage[q] = tmp[...].astype(BF16)

    for q in range(1, 16):
        send(stage.at[tp_ids[q]], cols.at[share_at(tp), :], bs.at[q], br.at[tp], (dp, tp_ids[q]))
    cols[share_at(tp), :] = stage[pl.ds(tp, 1)].reshape(share, 384)
    for q in range(1, 16):
        arrived(cols.at[share_at(tp_ids[q]), :], br.at[tp_ids[q]])

    lane = lax.broadcasted_iota(jnp.int32, (8, 128), 1)
    text_lane = lax.broadcasted_iota(jnp.int32, (128, 128), 1) >= T0

    def head(k, carry):
        ka = pl.ds(pl.multiple_of(k * 128, 128), 128)
        of_i = dot_nn(ent_i[ka, :], cols[:, 0:256])
        of_t = dot_nn(ent_t[ka, :], cols[...])
        hv[ka, 0:128] = jnp.where(text_lane, of_t[:, 0:128] + of_t[:, 128:256], of_i[:, 0:128] + of_i[:, 128:256])
        rest = of_t[:, 256:384]
        hv[ka, 128:256] = rest + pltpu.roll(rest, 96, 1)
        return carry

    lax.fori_loop(0, D // 128, head, 0)

    per = 128 // T2
    places = [(W + 8 * (j // per), T2 * (j % per)) for j in range(W // 8)]

    def pack(d):
        hp[d, 0:W, :] = hv[pl.ds(pl.multiple_of(d * W, 8), W), 0:128]
        packed = {}
        for j, (row, start) in enumerate(places):
            part = hv[pl.ds(pl.multiple_of(d * W + 8 * j, 8), 8), 128:256]
            if start:
                part = pltpu.roll(part, start, 1)
            packed[row] = jnp.where((lane >= start) & (lane < start + T2), part, packed.get(row, jnp.zeros((8, 128), F32)))
        for row, value in packed.items():
            hp[d, row : row + 8, :] = value

    for q in (8, 7, 9, 6, 10, 5, 11, 4, 12, 3, 13, 2, 14, 1, 15):
        to = (dp + q) % 16
        pack(to)
        send(hp.at[to], hv_got.at[16 - q], hs.at[q], hr.at[16 - q], (to, tp))
    pack(dp)
    total = hp[dp]
    for q in range(1, 16):
        arrived(hv_got.at[q], hr.at[q])
        total = total + hv_got[q]
    out_i[...] = total[0:W, 0:W]
    out_t[:, 0:T1] = pltpu.roll(total[0:W], T1, 1)[:, 0:T1]
    for j, (row, start) in enumerate(places):
        part = total[row : row + 8]
        if start:
            part = pltpu.roll(part, 128 - start, 1)
        out_t[8 * j : 8 * j + 8, T1:W] = part[:, 0:T2]
    for copy in started:
        copy.wait_send()


def solution(mesh):
    nz = mesh.shape["dp"] // 2
    nx = mesh.shape["tensor"] // 4

    def local(enc_i, enc_t, w_i, w_t, dw_i, dw_t, sharpness, offset):
        rows, D = enc_i.shape
        W = w_i.shape[1]
        share = rows // 16
        DX, DE = D + 128, 2 * D + 128
        vmem = pl.BlockSpec(memory_space=pltpu.VMEM)
        sem = lambda n: pltpu.SemaphoreType.DMA((n,))
        return pl.pallas_call(
            functools.partial(kernel, nz, nx, D, W),
            out_shape=[jax.ShapeDtypeStruct((W, W), F32)] * 2,
            in_specs=[pl.BlockSpec(memory_space=pl.ANY)] * 2 + [vmem] * 4 + [pl.BlockSpec(memory_space=pltpu.SMEM)] * 2,
            out_specs=[vmem] * 2,
            scratch_shapes=[
                pltpu.VMEM((rows, D), BF16),
                pltpu.VMEM((rows, D), BF16),
                sem(2),
                pltpu.VMEM((640, D), BF16),
                pltpu.VMEM((rows, 384), BF16),
                pltpu.VMEM((16, share, 384), BF16),
                pltpu.VMEM((4, share, D), F32),
                pltpu.VMEM((32 * share, DE), BF16),
                pltpu.VMEM((8 * share, DE), BF16),
                pltpu.VMEM((32 * share, DX), F32),
                pltpu.VMEM((32 * share, 4 * share), BF16),
                pltpu.VMEM((32 * share, 4 * share), BF16),
                pltpu.VMEM((8, 4 * share), F32),
                pltpu.VMEM((32 * share, DX), BF16),
                pltpu.VMEM((8 * share, DX), BF16),
                pltpu.VMEM((16 * share, DX), BF16),
                pltpu.VMEM((24, share, DX // 2), BF16),
                pltpu.VMEM((6, share, DX // 2), BF16),
                pltpu.VMEM((6, share, DX // 2), BF16),
                pltpu.VMEM((8, share, DX), BF16),
                pltpu.VMEM((16, share, 384), BF16),
                pltpu.VMEM((share, 384), F32),
                pltpu.VMEM((rows, 384), BF16),
                pltpu.VMEM((D, 256), F32),
                pltpu.VMEM((16, W + 16, 128), F32),
                pltpu.VMEM((16, W + 16, 128), F32),
                pltpu.VMEM((D, rows), BF16),
                pltpu.VMEM((D, rows), BF16),
            ]
            + [sem(n) for n in (16, 16, 64, 64, 8, 8, 4, 4, 32, 32, 8, 8, 16, 16, 16, 16)],
            compiler_params=pltpu.CompilerParams(
                collective_id=0, has_side_effects=True, vmem_limit_bytes=60 * 2**20
            ),
        )(enc_i, enc_t, w_i.T, w_t.T, dw_i.T, dw_t.T, sharpness, offset)

    in_specs = (
        P("dp", None),
        P("dp", None),
        P(None, "tensor"),
        P(None, "tensor"),
        P(None, "tensor"),
        P(None, "tensor"),
        P(),
        P(),
    )
    out_specs = (P("dp", "tensor"), P("dp", "tensor"))
    return jax.shard_map(local, mesh=mesh, in_specs=in_specs, out_specs=out_specs, check_vma=False)
```

```python
import functools

import jax
import jax.numpy as jnp
from jax import lax
from jax.experimental import pallas as pl
from jax.experimental.pallas import tpu as pltpu
from jax.sharding import PartitionSpec as P

EPS = 1e-06
MESH = pl.DeviceIdType.MESH
F32 = jnp.float32
BF16 = jnp.bfloat16

Z_SLOTS = (0, 3, -3, 4, 1, -1, 2, -2)
AWAY = (1, -1, 2)
XY_SLOTS = tuple(
    sorted(((i, j) for i in (0, 1, -1, 2) for j in (0, 1, -1, 2)), key=lambda p: abs(p[0]) + abs(p[1]))
)


def mirrored(back, period):
    return back if 2 * abs(back) == period else -back


def dot_nn(a, b):
    return lax.dot_general(a, b, (((1,), (0,)), ((), ())), preferred_element_type=F32)


def dot_nt(a, b):
    return lax.dot_general(a, b, (((1,), (1,)), ((), ())), preferred_element_type=F32)


def dot_tn(a, b):
    return lax.dot_general(a, b, (((0,), (0,)), ((), ())), preferred_element_type=F32)


def split_hi(value):
    hi = value.astype(BF16)
    lo = (value - hi.astype(F32)).astype(BF16)
    return hi, lo


def encoded(ends):
    lane = lax.broadcasted_iota(jnp.int32, ends.shape, 1)
    hi = ends.astype(BF16).astype(F32)
    lo = pltpu.roll(ends - hi, 2, 1)
    return jnp.where(lane < 2, hi, jnp.where(lane < 4, lo, 0.0)).astype(BF16)


def decoded(ends):
    ends = ends.astype(F32)
    return ends + pltpu.roll(ends, 126, 1)


def lanes_of(values, rows):
    lane = lax.broadcasted_iota(jnp.int32, (rows, 128), 1)
    out = jnp.zeros((rows, 128), F32)
    for index, value in enumerate(values):
        out = jnp.where(lane == index, value.astype(F32), out)
    return out


def kernel(
    nz, nx, D, W,
    from_i, from_t, w_i, w_t, dw_i, dw_t, sharpness, offset,
    out_i, out_t,
    enc_i, enc_t, cs, wpad, x_buf, x_got, raw, img, txt, gi, pb_buf, at_buf, csum,
    si_buf, st_buf, sib_got, first_got, next_buf, next_got, rt_buf, stage, tmp, cols, hv, hp, hv_got, ent_i, ent_t,
    fs, fr, ais, air, ats, atr, gs, gr, ris, rir, rts, rtr, bs, br, hs, hr,
):
    dp = lax.axis_index("dp")
    tp = lax.axis_index("tensor")
    z, h = dp // 2, dp % 2
    y, x, c = h * 2 + tp // (2 * nx), (tp // 2) % nx, tp % 2
    rows = enc_i.shape[0]
    share = rows // 16
    half = 16 * share
    DX = D + 128
    DE = 2 * D + 128
    T0 = 80
    T1 = 128 - T0
    T2 = W - T1
    s = sharpness[0]
    bias = offset[0]

    def device_at(dz, dy, dx, core):
        zz, yy, xx = (z - dz + nz) % nz, (y - dy + 4) % 4, (x - dx + nx) % nx
        return (zz * 2 + yy // 2, ((yy % 2) * nx + xx) * 2 + core)

    tp_ids = [(tp + q) % 16 for q in range(16)]
    z_ids = [device_at(b, 0, 0, c) for b in Z_SLOTS]
    xy_ids = [device_at(0, dy, dx, c) for dx, dy in XY_SLOTS]
    z_back = [Z_SLOTS.index(mirrored(b, nz)) for b in Z_SLOTS]
    xy_back = [XY_SLOTS.index((mirrored(dx, nx), mirrored(dy, 4))) for dx, dy in XY_SLOTS]

    started = []

    def send(src, dst, ssem, rsem, device):
        copy = pltpu.make_async_remote_copy(
            src_ref=src, dst_ref=dst, send_sem=ssem, recv_sem=rsem,
            device_id=device, device_id_type=MESH,
        )
        copy.start()
        started.append(copy)

    def arrived(dst, rsem):
        pltpu.make_async_remote_copy(
            src_ref=dst, dst_ref=dst, send_sem=fs.at[0], recv_sem=rsem,
            device_id=(dp, tp), device_id_type=MESH,
        ).wait_recv()

    loads = [pltpu.make_async_copy(a, b, cs.at[k]) for k, (a, b) in enumerate(((from_i, enc_i), (from_t, enc_t)))]
    for load in loads:
        load.start()

    barrier = pltpu.get_barrier_semaphore()
    peers = [(dp, tp_ids[q]) for q in range(1, 16)]
    peers += [(z * 2 + 1 - h, (tp + 2 * q) % 16) for q in range(8)]
    peers += [((dp + q) % 16, tp) for q in range(2, 15)]
    peers += [((dp + 15 - 14 * h) % 16, tp)]
    for peer in peers:
        pl.semaphore_signal(barrier, inc=1, device_id=peer, device_id_type=MESH)

    wpad[...] = jnp.zeros_like(wpad)
    wpad[0:W] = w_i[...]
    wpad[128 : 128 + W] = dw_i[...]
    wpad[256 + T0 : 384] = w_t[0:T1]
    wpad[384 + T0 : 512] = dw_t[0:T1]
    wpad[512 : 512 + T2] = w_t[T1:W]
    wpad[544 : 544 + T2] = dw_t[T1:W]

    def share_at(index):
        return pl.ds(pl.multiple_of(index * share, share), share)

    for load in loads:
        load.wait()

    for step in range(2):
        side = tp // 8 if step == 0 else 1 - tp // 8

        def project(r, carry):
            at = pl.ds(pl.multiple_of(side * (rows // 2) + r * (rows // 4), rows // 4), rows // 4)
            text = enc_t[at, :]
            x_buf[at, 0:256] = (dot_nt(enc_i[at, :], wpad[0:256]) + dot_nt(text, wpad[256:512])).astype(BF16)
            x_buf[at, 256:384] = dot_nt(text, wpad[512:640]).astype(BF16)
            return carry

        lax.fori_loop(0, 2, project, 0)
        if step == 0:
            pl.semaphore_wait(barrier, len(peers))
        for q in range(1 - step, 8):
            to = side * 8 + (tp + q) % 8
            send(x_buf.at[share_at(to), :], x_got.at[tp], fs.at[step * 8 + q], fr.at[tp], (dp, to))
    x_got[pl.ds(tp, 1)] = x_buf[share_at(tp), :].reshape(1, share, 384)
    for q in range(1, 16):
        arrived(x_got.at[tp_ids[q]], fr.at[tp_ids[q]])
    for q in range(16):
        last = x_got[q, :, 256:384].astype(F32)
        for k in range(2):
            tile = x_got[q, :, k * 128 : k * 128 + 128].astype(F32)
            raw[k, :, q * W : (q + 1) * W] = tile[:, 0:W]
            raw[2 + k, :, q * W : q * W + T1] = pltpu.roll(tile, T1, 1)[:, 0:T1]
            rest = last if k == 0 else pltpu.roll(last, 96, 1)
            raw[2 + k, :, q * W + T1 : (q + 1) * W] = rest[:, 0:T2]

    def unit_parts(values, tangent):
        radius = jnp.sqrt(jnp.sum(values * values, axis=1, keepdims=True) + EPS)
        inverse = 1.0 / radius
        unit = values * inverse
        rate = jnp.sum(unit * tangent, axis=1, keepdims=True)
        unit_tangent = (tangent - unit * rate) * inverse
        return unit, unit_tangent, inverse, rate * inverse

    for k, buf in ((0, img), (2, txt)):
        unit, tangent, inverse, ratio = unit_parts(raw[k], raw[k + 1])
        buf[0:share, 0:D] = unit.astype(BF16)
        buf[0:share, D : 2 * D] = tangent.astype(BF16)
        hi, lo = split_hi(ratio)
        buf[0:share, 2 * D : DE] = lanes_of((hi, lo), share).astype(BF16)

    parts = ((0, D), (D, DE - D))
    counts = {"i": 0, "t": 0}
    sib = (dp, tp + 1 - 2 * c)

    def ipart(slot, part):
        return img.at[pl.ds(slot * share, share), pl.ds(*parts[part])]

    def tat(slot):
        return txt.at[pl.ds(slot * share, share), :]

    def isend(src, dst, part, device):
        send(ipart(src, part), ipart(dst, part), ais.at[counts["i"]], air.at[part * 32 + dst], device)
        counts["i"] += 1

    def hop(pos, axis, way, part):
        to = list(pos)
        to[axis] = 2 if abs(pos[axis] + way) == 2 else pos[axis] + way
        away = [0, 0]
        away[axis] = -way
        isend(XY_SLOTS.index(pos), XY_SLOTS.index(tuple(to)), part, device_at(0, away[1], away[0], c))

    def i_on(pos, part):
        first, second = (0, 1) if part == 0 else (1, 0)
        if pos[second] == 0:
            if pos[first] >= 0 and (pos[first] == 0 or (part == 0 and pos[first] == 1)):
                hop(pos, first, 1, part)
            if pos[first] == 0 or (part == 1 and pos[first] == -1):
                hop(pos, first, -1, part)
            hop(pos, second, 1, part)
            hop(pos, second, -1, part)
        else:
            forth = pos[first] in (0, 2)
            if pos[second] == 1 and forth:
                hop(pos, second, 1, part)
            if pos[second] == -1 and not forth:
                hop(pos, second, -1, part)
        isend(XY_SLOTS.index(pos), 16 + XY_SLOTS.index(pos), part, sib)

    def i_step(pos):
        for part in (0, 1):
            slot = XY_SLOTS.index(pos)
            arrived(ipart(slot, part), air.at[part * 32 + slot])
            i_on(pos, part)

    def tsend(src, dst, device):
        send(tat(src), tat(dst), ats.at[counts["t"]], atr.at[dst], device)
        counts["t"] += 1

    def t_on(back):
        src = Z_SLOTS.index(back)
        if 0 <= back < 3:
            tsend(src, Z_SLOTS.index(back + 1), device_at(-1, 0, 0, c))
        if -3 < back <= 0:
            tsend(src, Z_SLOTS.index(back - 1), device_at(1, 0, 0, c))

    def twait(back):
        slot = Z_SLOTS.index(back)
        arrived(tat(slot), atr.at[slot])

    for part in (0, 1):
        i_on((0, 0), part)
    t_on(0)
    for k in range(D // 128):
        ka = pl.ds(k * 128, 128)
        ent_i[ka, :] = enc_i[:, ka].T
        ent_t[ka, :] = enc_t[:, ka].T
    eye = lanes_of([(lax.broadcasted_iota(jnp.int32, (8, 1), 0) == k) for k in range(8)], 8).astype(BF16)
    first_two = jnp.where(lax.broadcasted_iota(jnp.int32, (8, 128), 1) < 2, 1.0, 0.0).astype(BF16)
    TC = 4 * share
    RB = 8 * share

    def prepare(ci):
        csum[ci] = jnp.zeros((8, TC), F32)
        return dot_nt(first_two, txt[ci * TC : (ci + 1) * TC, 2 * D : DE])[0:1, :]

    def blocks(ci, sigma, low, high, first):
        at = pl.ds(ci * TC, TC)

        def block(r, carry):
            ra = pl.ds(pl.multiple_of(r * RB, RB), RB)
            tu = txt[at, 0:D]
            tt = txt[at, D : 2 * D]
            iu = img[ra, 0:D]
            it = img[ra, D : 2 * D]
            extra = img[ra, 2 * D : DE].astype(F32)
            rho = extra[:, 0:1] + extra[:, 1:2]
            cosine = dot_nt(iu, tu)
            cross = dot_nt(it, tu) + dot_nt(iu, tt)
            prob = jax.nn.sigmoid(s * cosine + bias)
            rate = prob * (1.0 - prob) * (s * cross)
            pb = prob.astype(BF16)
            q1 = prob * cosine
            q2 = prob * cross + rate * cosine
            csum[ci, 0:1, :] += jnp.sum(q1, axis=0, keepdims=True)
            csum[ci, 1:2, :] += jnp.sum(q2, axis=0, keepdims=True)
            pb_buf[ci, ra, :] = pb
            at_buf[ci, ra, :] = (rate - sigma * prob).astype(BF16)
            gain = dot_nn((rate - rho * prob).astype(BF16), tu) + dot_nn(pb, tt)
            sums = lanes_of((jnp.sum(q1, axis=1, keepdims=True), jnp.sum(q2, axis=1, keepdims=True)), RB)
            if first:
                gi[ra, 0:D] = gain
                gi[ra, D:DX] = sums
            else:
                gi[ra, 0:D] += gain
                gi[ra, D:DX] += sums
            return carry

        lax.fori_loop(low, high, block, 0)

    def text_sums(ci):
        at = pl.ds(ci * TC, TC)
        hi, lo = split_hi(csum[ci])
        tops = jnp.concatenate([hi[0:2].astype(F32), lo[0:2].astype(F32), jnp.zeros((4, TC), F32)], axis=0)
        st_buf[at, D:DX] = dot_tn(tops.astype(BF16), eye).astype(BF16)
        for k in range(0, D, 256):
            e = min(k + 256, D)
            gain = dot_tn(at_buf[ci], img[:, k:e]) + dot_tn(pb_buf[ci], img[:, D + k : D + e])
            st_buf[at, k:e] = gain.astype(BF16)
        for q in range(4 * ci, 4 * ci + 4):
            if q > 0:
                k = z_back[q]
                send(st_buf.at[pl.ds(q * share, share), :], rt_buf.at[k], rts.at[q], rtr.at[k], z_ids[q])

    def sums_out(row):
        at = pl.ds(row, share)
        si_buf[at, 0:D] = gi[at, 0:D].astype(BF16)
        si_buf[at, D:DX] = encoded(gi[at, D:DX])

    H = DX // 2
    halves = (pl.ds(0, H), pl.ds(H, H))
    counts["r"] = 0

    def rsend(src, dst, at, device):
        send(src, dst, ris.at[counts["r"]], rir.at[at], device)
        counts["r"] += 1

    def add_in(row, part, got):
        at = pl.ds(row, share)
        if part == 0:
            gi[at, 0:H] += got.astype(F32)
        else:
            gi[at, H:D] += got[:, 0 : D - H].astype(F32)
            gi[at, D:DX] += decoded(got[:, D - H : H])

    def to_sibling(first, last):
        for g in range(first, last):
            def one(q, carry):
                sums_out(pl.multiple_of(half + (4 * g + q) * share, share))
                return carry
            lax.fori_loop(0, 4, one, 0)
            src = si_buf.at[pl.ds(half + 4 * g * share, 4 * share), :]
            send(src, sib_got.at[pl.ds(4 * g * share, 4 * share), :], gs.at[g], gr.at[g], sib)

    for pos in XY_SLOTS[1:5]:
        i_step(pos)
    for back in (1, -1):
        twait(back)
        t_on(back)
    for pos in XY_SLOTS[5:8]:
        i_step(pos)
    for back in (2, -2):
        twait(back)
        t_on(back)
    near_sigma = prepare(1)
    blocks(1, near_sigma, 0, 1, True)
    for pos in XY_SLOTS[8:11]:
        i_step(pos)
    for back in (3, -3):
        twait(back)
    far = Z_SLOTS.index(3) + c * (Z_SLOTS.index(-3) - Z_SLOTS.index(3))
    tsend(far, Z_SLOTS.index(4), device_at(2 * c - 1, 0, 0, c))
    for pos in XY_SLOTS[11:15]:
        i_step(pos)
    twait(4)
    sigma = prepare(0)
    blocks(0, sigma, 0, 1, False)
    for pos in XY_SLOTS[15:16]:
        i_step(pos)
    blocks(1, near_sigma, 1, 2, True)
    blocks(0, sigma, 1, 2, False)
    for slot in range(16):
        for part in (0, 1):
            arrived(ipart(16 + slot, part), air.at[part * 32 + 16 + slot])
    blocks(0, sigma, 2, 4, True)
    text_sums(0)
    blocks(1, near_sigma, 2, 3, False)
    to_sibling(0, 2)
    blocks(1, near_sigma, 3, 4, False)
    to_sibling(2, 4)
    text_sums(1)

    near = (0,) + AWAY
    for g in range(4):
        arrived(sib_got.at[pl.ds(4 * g * share, 4 * share), :], gr.at[g])
        for q in range(4 * g, 4 * g + 4):
            qa = pl.ds(q * share, share)
            gi[qa, 0:D] += sib_got[qa, 0:D].astype(F32)
            gi[qa, D:DX] += decoded(sib_got[qa, D:DX])
            if q == 0:
                continue
            sums_out(q * share)
            dx, dy = XY_SLOTS[q]
            for part, off, keep in ((0, dy, dx), (1, dx, dy)):
                if off:
                    at = part * 12 + AWAY.index(mirrored(off, 4)) * 4 + near.index(keep)
                    to = device_at(0, dy, 0, c) if part == 0 else device_at(0, 0, dx, c)
                    rsend(si_buf.at[qa, halves[part]], first_got.at[at], at, to)
    for keep in AWAY + (0,):
        for part in (0, 1):
            row = XY_SLOTS.index((keep, 0) if part == 0 else (0, keep)) * share
            for o in range(3):
                at = part * 12 + o * 4 + near.index(keep)
                arrived(first_got.at[at], rir.at[at])
                add_in(row, part, first_got[at])
            if keep == 0:
                continue
            at = part * 3 + AWAY.index(keep)
            ra = pl.ds(row, share)
            if part == 0:
                next_buf[at] = gi[ra, 0:H].astype(BF16)
                to = device_at(0, 0, keep, c)
            else:
                next_buf[at, :, 0 : D - H] = gi[ra, H:D].astype(BF16)
                next_buf[at, :, D - H : H] = encoded(gi[ra, D:DX])
                to = device_at(0, keep, 0, c)
            k = part * 3 + AWAY.index(mirrored(keep, 4))
            rsend(next_buf.at[at], next_got.at[k], 24 + k, to)

    for q in range(1, 8):
        arrived(rt_buf.at[q], rtr.at[q])
    iu, it = img[0:share, 0:D].astype(F32), img[0:share, D : 2 * D].astype(F32)
    tu, tt = txt[0:share, 0:D].astype(F32), txt[0:share, D : 2 * D].astype(F32)
    pair_cos = jnp.sum(iu * tu, axis=1, keepdims=True)
    pair_cross = jnp.sum(it * tu + iu * tt, axis=1, keepdims=True)
    tmp[...] = jnp.zeros_like(tmp)
    for k in (1, 0):
        if k == 0:
            for q in range(6):
                arrived(next_got.at[q], rir.at[24 + q])
                add_in(0, q // 3, next_got[q])
            total = gi[0:share, 0:D]
            inner = gi[0:share, D : D + 1]
            inner_rate = gi[0:share, D + 1 : D + 2]
            more = []
            other, other_tangent = tu, tt
        else:
            total, inner, inner_rate = 0.0, 0.0, 0.0
            more = [st_buf[0:share, :]] + [rt_buf[q] for q in range(1, 8)]
            other, other_tangent = iu, it
        for term in more:
            total = total + term[:, 0:D].astype(F32)
            ends = term[:, D:DX].astype(F32)
            inner = inner + (ends[:, 0:1] + ends[:, 2:3])
            inner_rate = inner_rate + (ends[:, 1:2] + ends[:, 3:4])
        unit, tangent, inverse, ratio = unit_parts(raw[2 * k], raw[2 * k + 1])
        total = s * (total + (ratio * other - other_tangent))
        inner = s * (inner - pair_cos)
        inner_rate = s * (inner_rate - pair_cross)
        back = (total - tangent * inner - unit * (inner_rate - ratio * inner)) * inverse
        hi, lo = split_hi(back)
        raw[2 * k] = hi.astype(F32)
        raw[2 * k + 1] = lo.astype(F32)
    for q in range(16):
        for k in range(2):
            tmp[:, k * 128 : k * 128 + W] = raw[k, :, q * W : (q + 1) * W]
            tmp[:, k * 128 + T0 : k * 128 + 128] = raw[2 + k, :, q * W : q * W + T1]
            tmp[:, 256 + 32 * k : 256 + 32 * k + T2] = raw[2 + k, :, q * W + T1 : (q + 1) * W]
        stage[q] = tmp[...].astype(BF16)

    for q in range(1, 16):
        send(stage.at[tp_ids[q]], cols.at[share_at(tp), :], bs.at[q], br.at[tp], (dp, tp_ids[q]))
    cols[share_at(tp), :] = stage[pl.ds(tp, 1)].reshape(share, 384)
    for q in range(1, 16):
        arrived(cols.at[share_at(tp_ids[q]), :], br.at[tp_ids[q]])

    lane = lax.broadcasted_iota(jnp.int32, (8, 128), 1)
    text_lane = lax.broadcasted_iota(jnp.int32, (128, 128), 1) >= T0

    def head(k, carry):
        ka = pl.ds(pl.multiple_of(k * 128, 128), 128)
        of_i = dot_nn(ent_i[ka, :], cols[:, 0:256])
        of_t = dot_nn(ent_t[ka, :], cols[...])
        hv[ka, 0:128] = jnp.where(text_lane, of_t[:, 0:128] + of_t[:, 128:256], of_i[:, 0:128] + of_i[:, 128:256])
        rest = of_t[:, 256:384]
        hv[ka, 128:256] = rest + pltpu.roll(rest, 96, 1)
        return carry

    lax.fori_loop(0, D // 128, head, 0)

    per = 128 // T2
    places = [(W + 8 * (j // per), T2 * (j % per)) for j in range(W // 8)]

    def pack(d):
        hp[d, 0:W, :] = hv[pl.ds(pl.multiple_of(d * W, 8), W), 0:128]
        packed = {}
        for j, (row, start) in enumerate(places):
            part = hv[pl.ds(pl.multiple_of(d * W + 8 * j, 8), 8), 128:256]
            if start:
                part = pltpu.roll(part, start, 1)
            packed[row] = jnp.where((lane >= start) & (lane < start + T2), part, packed.get(row, jnp.zeros((8, 128), F32)))
        for row, value in packed.items():
            hp[d, row : row + 8, :] = value

    for q in (8, 7, 9, 6, 10, 5, 11, 4, 12, 3, 13, 2, 14, 1, 15):
        to = (dp + q) % 16
        pack(to)
        send(hp.at[to], hv_got.at[16 - q], hs.at[q], hr.at[16 - q], (to, tp))
    pack(dp)
    total = hp[dp]
    for q in range(1, 16):
        arrived(hv_got.at[q], hr.at[q])
        total = total + hv_got[q]
    out_i[...] = total[0:W, 0:W]
    out_t[:, 0:T1] = pltpu.roll(total[0:W], T1, 1)[:, 0:T1]
    for j, (row, start) in enumerate(places):
        part = total[row : row + 8]
        if start:
            part = pltpu.roll(part, 128 - start, 1)
        out_t[8 * j : 8 * j + 8, T1:W] = part[:, 0:T2]
    for copy in started:
        copy.wait_send()


def solution(mesh):
    nz = mesh.shape["dp"] // 2
    nx = mesh.shape["tensor"] // 4

    def local(enc_i, enc_t, w_i, w_t, dw_i, dw_t, sharpness, offset):
        rows, D = enc_i.shape
        W = w_i.shape[1]
        share = rows // 16
        DX, DE = D + 128, 2 * D + 128
        vmem = pl.BlockSpec(memory_space=pltpu.VMEM)
        sem = lambda n: pltpu.SemaphoreType.DMA((n,))
        return pl.pallas_call(
            functools.partial(kernel, nz, nx, D, W),
            out_shape=[jax.ShapeDtypeStruct((W, W), F32)] * 2,
            in_specs=[pl.BlockSpec(memory_space=pl.ANY)] * 2 + [vmem] * 4 + [pl.BlockSpec(memory_space=pltpu.SMEM)] * 2,
            out_specs=[vmem] * 2,
            scratch_shapes=[
                pltpu.VMEM((rows, D), BF16),
                pltpu.VMEM((rows, D), BF16),
                sem(2),
                pltpu.VMEM((640, D), BF16),
                pltpu.VMEM((rows, 384), BF16),
                pltpu.VMEM((16, share, 384), BF16),
                pltpu.VMEM((4, share, D), F32),
                pltpu.VMEM((32 * share, DE), BF16),
                pltpu.VMEM((8 * share, DE), BF16),
                pltpu.VMEM((32 * share, DX), F32),
                pltpu.VMEM((2, 32 * share, 4 * share), BF16),
                pltpu.VMEM((2, 32 * share, 4 * share), BF16),
                pltpu.VMEM((2, 8, 4 * share), F32),
                pltpu.VMEM((32 * share, DX), BF16),
                pltpu.VMEM((8 * share, DX), BF16),
                pltpu.VMEM((16 * share, DX), BF16),
                pltpu.VMEM((24, share, DX // 2), BF16),
                pltpu.VMEM((6, share, DX // 2), BF16),
                pltpu.VMEM((6, share, DX // 2), BF16),
                pltpu.VMEM((8, share, DX), BF16),
                pltpu.VMEM((16, share, 384), BF16),
                pltpu.VMEM((share, 384), F32),
                pltpu.VMEM((rows, 384), BF16),
                pltpu.VMEM((D, 256), F32),
                pltpu.VMEM((16, W + 16, 128), F32),
                pltpu.VMEM((16, W + 16, 128), F32),
                pltpu.VMEM((D, rows), BF16),
                pltpu.VMEM((D, rows), BF16),
            ]
            + [sem(n) for n in (16, 16, 64, 64, 8, 8, 4, 4, 32, 32, 8, 8, 16, 16, 16, 16)],
            compiler_params=pltpu.CompilerParams(
                collective_id=0, has_side_effects=True, vmem_limit_bytes=60 * 2**20
            ),
        )(enc_i, enc_t, w_i.T, w_t.T, dw_i.T, dw_t.T, sharpness, offset)

    in_specs = (
        P("dp", None),
        P("dp", None),
        P(None, "tensor"),
        P(None, "tensor"),
        P(None, "tensor"),
        P(None, "tensor"),
        P(),
        P(),
    )
    out_specs = (P("dp", "tensor"), P("dp", "tensor"))
    return jax.shard_map(local, mesh=mesh, in_specs=in_specs, out_specs=out_specs, check_vma=False)
```

```python
import functools

import jax
import jax.numpy as jnp
from jax import lax
from jax.experimental import pallas as pl
from jax.experimental.pallas import tpu as pltpu
from jax.sharding import PartitionSpec as P

EPS = 1e-06
MESH = pl.DeviceIdType.MESH
F32 = jnp.float32
BF16 = jnp.bfloat16

Z_SLOTS = (0, 3, -3, 4, 1, -1, 2, -2)
AWAY = (1, -1, 2)
XY_SLOTS = tuple(
    sorted(((i, j) for i in (0, 1, -1, 2) for j in (0, 1, -1, 2)), key=lambda p: abs(p[0]) + abs(p[1]))
)


def mirrored(back, period):
    return back if 2 * abs(back) == period else -back


def dot_nn(a, b):
    return lax.dot_general(a, b, (((1,), (0,)), ((), ())), preferred_element_type=F32)


def dot_nt(a, b):
    return lax.dot_general(a, b, (((1,), (1,)), ((), ())), preferred_element_type=F32)


def dot_tn(a, b):
    return lax.dot_general(a, b, (((0,), (0,)), ((), ())), preferred_element_type=F32)


def split_hi(value):
    hi = value.astype(BF16)
    lo = (value - hi.astype(F32)).astype(BF16)
    return hi, lo


def encoded(ends):
    lane = lax.broadcasted_iota(jnp.int32, ends.shape, 1)
    hi = ends.astype(BF16).astype(F32)
    lo = pltpu.roll(ends - hi, 2, 1)
    return jnp.where(lane < 2, hi, jnp.where(lane < 4, lo, 0.0)).astype(BF16)


def decoded(ends):
    ends = ends.astype(F32)
    return ends + pltpu.roll(ends, 126, 1)


def lanes_of(values, rows):
    lane = lax.broadcasted_iota(jnp.int32, (rows, 128), 1)
    out = jnp.zeros((rows, 128), F32)
    for index, value in enumerate(values):
        out = jnp.where(lane == index, value.astype(F32), out)
    return out


def kernel(
    nz, nx, D, W,
    from_i, from_t, w_i, w_t, dw_i, dw_t, sharpness, offset,
    out_i, out_t,
    enc_i, enc_t, cs, wpad, x_buf, x_got, raw, img, txt, gi, pb_buf, at_buf, csum,
    si_buf, st_buf, sib_got, first_got, next_buf, next_got, rt_buf, stage, tmp, cols, hv, hp, hv_got, ent_i, ent_t,
    fs, fr, ais, air, ats, atr, gs, gr, ris, rir, rts, rtr, bs, br, hs, hr,
):
    dp = lax.axis_index("dp")
    tp = lax.axis_index("tensor")
    z, h = dp // 2, dp % 2
    y, x, c = h * 2 + tp // (2 * nx), (tp // 2) % nx, tp % 2
    rows = enc_i.shape[0]
    share = rows // 16
    half = 16 * share
    DX = D + 128
    DE = 2 * D + 128
    T0 = 80
    T1 = 128 - T0
    T2 = W - T1
    s = sharpness[0]
    bias = offset[0]

    def device_at(dz, dy, dx, core):
        zz, yy, xx = (z - dz + nz) % nz, (y - dy + 4) % 4, (x - dx + nx) % nx
        return (zz * 2 + yy // 2, ((yy % 2) * nx + xx) * 2 + core)

    tp_ids = [(tp + q) % 16 for q in range(16)]
    z_ids = [device_at(b, 0, 0, c) for b in Z_SLOTS]
    xy_ids = [device_at(0, dy, dx, c) for dx, dy in XY_SLOTS]
    z_back = [Z_SLOTS.index(mirrored(b, nz)) for b in Z_SLOTS]
    xy_back = [XY_SLOTS.index((mirrored(dx, nx), mirrored(dy, 4))) for dx, dy in XY_SLOTS]

    started = []

    def send(src, dst, ssem, rsem, device):
        copy = pltpu.make_async_remote_copy(
            src_ref=src, dst_ref=dst, send_sem=ssem, recv_sem=rsem,
            device_id=device, device_id_type=MESH,
        )
        copy.start()
        started.append(copy)

    def arrived(dst, rsem):
        pltpu.make_async_remote_copy(
            src_ref=dst, dst_ref=dst, send_sem=fs.at[0], recv_sem=rsem,
            device_id=(dp, tp), device_id_type=MESH,
        ).wait_recv()

    loads = [pltpu.make_async_copy(a, b, cs.at[k]) for k, (a, b) in enumerate(((from_i, enc_i), (from_t, enc_t)))]
    for load in loads:
        load.start()

    barrier = pltpu.get_barrier_semaphore()
    peers = [(dp, tp_ids[q]) for q in range(1, 16)]
    peers += [(z * 2 + 1 - h, (tp + 2 * q) % 16) for q in range(8)]
    peers += [((dp + q) % 16, tp) for q in range(2, 15)]
    peers += [((dp + 15 - 14 * h) % 16, tp)]
    for peer in peers:
        pl.semaphore_signal(barrier, inc=1, device_id=peer, device_id_type=MESH)

    wpad[...] = jnp.zeros_like(wpad)
    wpad[0:W] = w_i[...]
    wpad[128 : 128 + W] = dw_i[...]
    wpad[256 + T0 : 384] = w_t[0:T1]
    wpad[384 + T0 : 512] = dw_t[0:T1]
    wpad[512 : 512 + T2] = w_t[T1:W]
    wpad[544 : 544 + T2] = dw_t[T1:W]

    def share_at(index):
        return pl.ds(pl.multiple_of(index * share, share), share)

    for load in loads:
        load.wait()

    for step in range(2):
        side = tp // 8 if step == 0 else 1 - tp // 8

        def project(r, carry):
            at = pl.ds(pl.multiple_of(side * (rows // 2) + r * (rows // 4), rows // 4), rows // 4)
            text = enc_t[at, :]
            x_buf[at, 0:256] = (dot_nt(enc_i[at, :], wpad[0:256]) + dot_nt(text, wpad[256:512])).astype(BF16)
            x_buf[at, 256:384] = dot_nt(text, wpad[512:640]).astype(BF16)
            return carry

        lax.fori_loop(0, 2, project, 0)
        if step == 0:
            pl.semaphore_wait(barrier, len(peers))
        for q in range(1 - step, 8):
            to = side * 8 + (tp + q) % 8
            send(x_buf.at[share_at(to), :], x_got.at[tp], fs.at[step * 8 + q], fr.at[tp], (dp, to))
    x_got[pl.ds(tp, 1)] = x_buf[share_at(tp), :].reshape(1, share, 384)
    for q in range(1, 16):
        arrived(x_got.at[tp_ids[q]], fr.at[tp_ids[q]])
    for q in range(16):
        last = x_got[q, :, 256:384].astype(F32)
        for k in range(2):
            tile = x_got[q, :, k * 128 : k * 128 + 128].astype(F32)
            raw[k, :, q * W : (q + 1) * W] = tile[:, 0:W]
            raw[2 + k, :, q * W : q * W + T1] = pltpu.roll(tile, T1, 1)[:, 0:T1]
            rest = last if k == 0 else pltpu.roll(last, 96, 1)
            raw[2 + k, :, q * W + T1 : (q + 1) * W] = rest[:, 0:T2]

    def unit_parts(values, tangent):
        radius = jnp.sqrt(jnp.sum(values * values, axis=1, keepdims=True) + EPS)
        inverse = 1.0 / radius
        unit = values * inverse
        rate = jnp.sum(unit * tangent, axis=1, keepdims=True)
        unit_tangent = (tangent - unit * rate) * inverse
        return unit, unit_tangent, inverse, rate * inverse

    for k, buf in ((0, img), (2, txt)):
        unit, tangent, inverse, ratio = unit_parts(raw[k], raw[k + 1])
        buf[0:share, 0:D] = unit.astype(BF16)
        buf[0:share, D : 2 * D] = tangent.astype(BF16)
        hi, lo = split_hi(ratio)
        buf[0:share, 2 * D : DE] = lanes_of((hi, lo), share).astype(BF16)

    parts = ((0, D), (D, DE - D))
    counts = {"i": 0, "t": 0}
    sib = (dp, tp + 1 - 2 * c)

    def ipart(slot, part):
        return img.at[pl.ds(slot * share, share), pl.ds(*parts[part])]

    def tat(slot):
        return txt.at[pl.ds(slot * share, share), :]

    def isend(src, dst, part, device):
        send(ipart(src, part), ipart(dst, part), ais.at[counts["i"]], air.at[part * 32 + dst], device)
        counts["i"] += 1

    def hop(pos, axis, way, part):
        to = list(pos)
        to[axis] = 2 if abs(pos[axis] + way) == 2 else pos[axis] + way
        away = [0, 0]
        away[axis] = -way
        isend(XY_SLOTS.index(pos), XY_SLOTS.index(tuple(to)), part, device_at(0, away[1], away[0], c))

    def i_on(pos, part):
        first, second = (0, 1) if part == 0 else (1, 0)
        if pos[second] == 0:
            if pos[first] >= 0 and (pos[first] == 0 or (part == 0 and pos[first] == 1)):
                hop(pos, first, 1, part)
            if pos[first] == 0 or (part == 1 and pos[first] == -1):
                hop(pos, first, -1, part)
            hop(pos, second, 1, part)
            hop(pos, second, -1, part)
        else:
            forth = pos[first] in (0, 2)
            if pos[second] == 1 and forth:
                hop(pos, second, 1, part)
            if pos[second] == -1 and not forth:
                hop(pos, second, -1, part)
        isend(XY_SLOTS.index(pos), 16 + XY_SLOTS.index(pos), part, sib)

    def i_step(pos):
        for part in (0, 1):
            slot = XY_SLOTS.index(pos)
            arrived(ipart(slot, part), air.at[part * 32 + slot])
            i_on(pos, part)

    def tsend(src, dst, device):
        send(tat(src), tat(dst), ats.at[counts["t"]], atr.at[dst], device)
        counts["t"] += 1

    def t_on(back):
        src = Z_SLOTS.index(back)
        if 0 <= back < 3:
            tsend(src, Z_SLOTS.index(back + 1), device_at(-1, 0, 0, c))
        if -3 < back <= 0:
            tsend(src, Z_SLOTS.index(back - 1), device_at(1, 0, 0, c))

    def twait(back):
        slot = Z_SLOTS.index(back)
        arrived(tat(slot), atr.at[slot])

    for part in (0, 1):
        i_on((0, 0), part)
    t_on(0)
    for k in range(D // 128):
        ka = pl.ds(k * 128, 128)
        ent_i[ka, :] = enc_i[:, ka].T
        ent_t[ka, :] = enc_t[:, ka].T
    eye = lanes_of([(lax.broadcasted_iota(jnp.int32, (8, 1), 0) == k) for k in range(8)], 8).astype(BF16)
    first_two = jnp.where(lax.broadcasted_iota(jnp.int32, (8, 128), 1) < 2, 1.0, 0.0).astype(BF16)
    TC = 4 * share
    RB = 8 * share

    def prepare(ci):
        csum[ci] = jnp.zeros((8, TC), F32)
        return dot_nt(first_two, txt[ci * TC : (ci + 1) * TC, 2 * D : DE])[0:1, :]

    def blocks(ci, sigma, low, high, first):
        at = pl.ds(ci * TC, TC)

        def block(r, carry):
            ra = pl.ds(pl.multiple_of(r * RB, RB), RB)
            tu = txt[at, 0:D]
            tt = txt[at, D : 2 * D]
            iu = img[ra, 0:D]
            it = img[ra, D : 2 * D]
            extra = img[ra, 2 * D : DE].astype(F32)
            rho = extra[:, 0:1] + extra[:, 1:2]
            cosine = dot_nt(iu, tu)
            cross = dot_nt(it, tu) + dot_nt(iu, tt)
            prob = jax.nn.sigmoid(s * cosine + bias)
            rate = prob * (1.0 - prob) * (s * cross)
            pb = prob.astype(BF16)
            q1 = prob * cosine
            q2 = prob * cross + rate * cosine
            csum[ci, 0:1, :] += jnp.sum(q1, axis=0, keepdims=True)
            csum[ci, 1:2, :] += jnp.sum(q2, axis=0, keepdims=True)
            pb_buf[ci, ra, :] = pb
            at_buf[ci, ra, :] = (rate - sigma * prob).astype(BF16)
            gain = dot_nn((rate - rho * prob).astype(BF16), tu) + dot_nn(pb, tt)
            sums = lanes_of((jnp.sum(q1, axis=1, keepdims=True), jnp.sum(q2, axis=1, keepdims=True)), RB)
            if first:
                gi[ra, 0:D] = gain
                gi[ra, D:DX] = sums
            else:
                gi[ra, 0:D] += gain
                gi[ra, D:DX] += sums
            return carry

        lax.fori_loop(low, high, block, 0)

    def text_sums(ci):
        at = pl.ds(ci * TC, TC)
        hi, lo = split_hi(csum[ci])
        tops = jnp.concatenate([hi[0:2].astype(F32), lo[0:2].astype(F32), jnp.zeros((4, TC), F32)], axis=0)
        st_buf[at, D:DX] = dot_tn(tops.astype(BF16), eye).astype(BF16)
        for k in range(0, D, 256):
            e = min(k + 256, D)
            gain = dot_tn(at_buf[ci], img[:, k:e]) + dot_tn(pb_buf[ci], img[:, D + k : D + e])
            st_buf[at, k:e] = gain.astype(BF16)
        for q in range(4 * ci, 4 * ci + 4):
            if q > 0:
                k = z_back[q]
                send(st_buf.at[pl.ds(q * share, share), :], rt_buf.at[k], rts.at[q], rtr.at[k], z_ids[q])

    def sums_out(row):
        at = pl.ds(row, share)
        si_buf[at, 0:D] = gi[at, 0:D].astype(BF16)
        si_buf[at, D:DX] = encoded(gi[at, D:DX])

    H = DX // 2
    halves = (pl.ds(0, H), pl.ds(H, H))
    counts["r"] = 0

    def rsend(src, dst, at, device):
        send(src, dst, ris.at[counts["r"]], rir.at[at], device)
        counts["r"] += 1

    def add_in(row, part, got):
        at = pl.ds(row, share)
        if part == 0:
            gi[at, 0:H] += got.astype(F32)
        else:
            gi[at, H:D] += got[:, 0 : D - H].astype(F32)
            gi[at, D:DX] += decoded(got[:, D - H : H])

    def to_sibling(first, last):
        for g in range(first, last):
            def one(q, carry):
                sums_out(pl.multiple_of(half + (4 * g + q) * share, share))
                return carry
            lax.fori_loop(0, 4, one, 0)
            src = si_buf.at[pl.ds(half + 4 * g * share, 4 * share), :]
            send(src, sib_got.at[pl.ds(4 * g * share, 4 * share), :], gs.at[g], gr.at[g], sib)

    for pos in XY_SLOTS[1:5]:
        i_step(pos)
    for back in (1, -1):
        twait(back)
        t_on(back)
    for pos in XY_SLOTS[5:8]:
        i_step(pos)
    for back in (2, -2):
        twait(back)
        t_on(back)
    near_sigma = prepare(1)
    blocks(1, near_sigma, 0, 1, True)
    for pos in XY_SLOTS[8:11]:
        i_step(pos)
    for back in (3, -3):
        twait(back)
    far = Z_SLOTS.index(3) + c * (Z_SLOTS.index(-3) - Z_SLOTS.index(3))
    tsend(far, Z_SLOTS.index(4), device_at(2 * c - 1, 0, 0, c))
    for pos in XY_SLOTS[11:15]:
        i_step(pos)
    twait(4)
    sigma = prepare(0)
    blocks(0, sigma, 0, 1, False)
    for pos in XY_SLOTS[15:16]:
        i_step(pos)
    blocks(1, near_sigma, 1, 2, True)
    blocks(0, sigma, 1, 2, False)
    for slot in range(16):
        for part in (0, 1):
            arrived(ipart(16 + slot, part), air.at[part * 32 + 16 + slot])
    blocks(0, sigma, 2, 4, True)
    text_sums(0)
    blocks(1, near_sigma, 2, 3, False)
    to_sibling(0, 2)
    blocks(1, near_sigma, 3, 4, False)
    to_sibling(2, 4)
    text_sums(1)

    near = (0,) + AWAY
    for g in range(4):
        arrived(sib_got.at[pl.ds(4 * g * share, 4 * share), :], gr.at[g])
        for q in range(4 * g, 4 * g + 4):
            qa = pl.ds(q * share, share)
            gi[qa, 0:D] += sib_got[qa, 0:D].astype(F32)
            gi[qa, D:DX] += decoded(sib_got[qa, D:DX])
            if q == 0:
                continue
            sums_out(q * share)
            dx, dy = XY_SLOTS[q]
            for part, off, keep in ((0, dy, dx), (1, dx, dy)):
                if off:
                    at = part * 12 + AWAY.index(mirrored(off, 4)) * 4 + near.index(keep)
                    to = device_at(0, dy, 0, c) if part == 0 else device_at(0, 0, dx, c)
                    rsend(si_buf.at[qa, halves[part]], first_got.at[at], at, to)
    for keep in AWAY + (0,):
        for part in (0, 1):
            row = XY_SLOTS.index((keep, 0) if part == 0 else (0, keep)) * share
            for o in range(3):
                at = part * 12 + o * 4 + near.index(keep)
                arrived(first_got.at[at], rir.at[at])
                add_in(row, part, first_got[at])
            if keep == 0:
                continue
            at = part * 3 + AWAY.index(keep)
            ra = pl.ds(row, share)
            if part == 0:
                next_buf[at] = gi[ra, 0:H].astype(BF16)
                to = device_at(0, 0, keep, c)
            else:
                next_buf[at, :, 0 : D - H] = gi[ra, H:D].astype(BF16)
                next_buf[at, :, D - H : H] = encoded(gi[ra, D:DX])
                to = device_at(0, keep, 0, c)
            k = part * 3 + AWAY.index(mirrored(keep, 4))
            rsend(next_buf.at[at], next_got.at[k], 24 + k, to)

    for q in range(1, 8):
        arrived(rt_buf.at[q], rtr.at[q])
    iu, it = img[0:share, 0:D].astype(F32), img[0:share, D : 2 * D].astype(F32)
    tu, tt = txt[0:share, 0:D].astype(F32), txt[0:share, D : 2 * D].astype(F32)
    pair_cos = jnp.sum(iu * tu, axis=1, keepdims=True)
    pair_cross = jnp.sum(it * tu + iu * tt, axis=1, keepdims=True)
    tmp[...] = jnp.zeros_like(tmp)
    for k in (1, 0):
        if k == 0:
            for q in range(6):
                arrived(next_got.at[q], rir.at[24 + q])
                add_in(0, q // 3, next_got[q])
            total = gi[0:share, 0:D]
            inner = gi[0:share, D : D + 1]
            inner_rate = gi[0:share, D + 1 : D + 2]
            more = []
            other, other_tangent = tu, tt
        else:
            total, inner, inner_rate = 0.0, 0.0, 0.0
            more = [st_buf[0:share, :]] + [rt_buf[q] for q in range(1, 8)]
            other, other_tangent = iu, it
        for term in more:
            total = total + term[:, 0:D].astype(F32)
            ends = term[:, D:DX].astype(F32)
            inner = inner + (ends[:, 0:1] + ends[:, 2:3])
            inner_rate = inner_rate + (ends[:, 1:2] + ends[:, 3:4])
        unit, tangent, inverse, ratio = unit_parts(raw[2 * k], raw[2 * k + 1])
        total = s * (total + (ratio * other - other_tangent))
        inner = s * (inner - pair_cos)
        inner_rate = s * (inner_rate - pair_cross)
        back = (total - tangent * inner - unit * (inner_rate - ratio * inner)) * inverse
        hi, lo = split_hi(back)
        raw[2 * k] = hi.astype(F32)
        raw[2 * k + 1] = lo.astype(F32)
    for q in range(16):
        for k in range(2):
            tmp[:, k * 128 : k * 128 + W] = raw[k, :, q * W : (q + 1) * W]
            tmp[:, k * 128 + T0 : k * 128 + 128] = raw[2 + k, :, q * W : q * W + T1]
            tmp[:, 256 + 32 * k : 256 + 32 * k + T2] = raw[2 + k, :, q * W + T1 : (q + 1) * W]
        stage[q] = tmp[...].astype(BF16)

    for step in range(2):
        side = 1 - tp // 8 if step == 0 else tp // 8
        for q in range(step, 8):
            to = side * 8 + (tp + q) % 8
            send(stage.at[to], cols.at[share_at(tp), :], bs.at[step * 8 + q], br.at[tp], (dp, to))
    cols[share_at(tp), :] = stage[pl.ds(tp, 1)].reshape(share, 384)
    for q in range(1, 16):
        arrived(cols.at[share_at(tp_ids[q]), :], br.at[tp_ids[q]])

    lane = lax.broadcasted_iota(jnp.int32, (8, 128), 1)
    text_lane = lax.broadcasted_iota(jnp.int32, (128, 128), 1) >= T0

    def head(k, carry):
        ka = pl.ds(pl.multiple_of(k * 128, 128), 128)
        of_i = dot_nn(ent_i[ka, :], cols[:, 0:256])
        of_t = dot_nn(ent_t[ka, :], cols[...])
        hv[ka, 0:128] = jnp.where(text_lane, of_t[:, 0:128] + of_t[:, 128:256], of_i[:, 0:128] + of_i[:, 128:256])
        rest = of_t[:, 256:384]
        hv[ka, 128:256] = rest + pltpu.roll(rest, 96, 1)
        return carry

    lax.fori_loop(0, D // 128, head, 0)

    per = 128 // T2
    places = [(W + 8 * (j // per), T2 * (j % per)) for j in range(W // 8)]

    def pack(d):
        hp[d, 0:W, :] = hv[pl.ds(pl.multiple_of(d * W, 8), W), 0:128]
        packed = {}
        for j, (row, start) in enumerate(places):
            part = hv[pl.ds(pl.multiple_of(d * W + 8 * j, 8), 8), 128:256]
            if start:
                part = pltpu.roll(part, start, 1)
            packed[row] = jnp.where((lane >= start) & (lane < start + T2), part, packed.get(row, jnp.zeros((8, 128), F32)))
        for row, value in packed.items():
            hp[d, row : row + 8, :] = value

    for q in (8, 7, 9, 6, 10, 5, 11, 4, 12, 3, 13, 2, 14, 1, 15):
        to = (dp + q) % 16
        pack(to)
        send(hp.at[to], hv_got.at[16 - q], hs.at[q], hr.at[16 - q], (to, tp))
    pack(dp)
    total = hp[dp]
    for q in range(1, 16):
        arrived(hv_got.at[q], hr.at[q])
        total = total + hv_got[q]
    out_i[...] = total[0:W, 0:W]
    out_t[:, 0:T1] = pltpu.roll(total[0:W], T1, 1)[:, 0:T1]
    for j, (row, start) in enumerate(places):
        part = total[row : row + 8]
        if start:
            part = pltpu.roll(part, 128 - start, 1)
        out_t[8 * j : 8 * j + 8, T1:W] = part[:, 0:T2]
    for copy in started:
        copy.wait_send()


def solution(mesh):
    nz = mesh.shape["dp"] // 2
    nx = mesh.shape["tensor"] // 4

    def local(enc_i, enc_t, w_i, w_t, dw_i, dw_t, sharpness, offset):
        rows, D = enc_i.shape
        W = w_i.shape[1]
        share = rows // 16
        DX, DE = D + 128, 2 * D + 128
        vmem = pl.BlockSpec(memory_space=pltpu.VMEM)
        sem = lambda n: pltpu.SemaphoreType.DMA((n,))
        return pl.pallas_call(
            functools.partial(kernel, nz, nx, D, W),
            out_shape=[jax.ShapeDtypeStruct((W, W), F32)] * 2,
            in_specs=[pl.BlockSpec(memory_space=pl.ANY)] * 2 + [vmem] * 4 + [pl.BlockSpec(memory_space=pltpu.SMEM)] * 2,
            out_specs=[vmem] * 2,
            scratch_shapes=[
                pltpu.VMEM((rows, D), BF16),
                pltpu.VMEM((rows, D), BF16),
                sem(2),
                pltpu.VMEM((640, D), BF16),
                pltpu.VMEM((rows, 384), BF16),
                pltpu.VMEM((16, share, 384), BF16),
                pltpu.VMEM((4, share, D), F32),
                pltpu.VMEM((32 * share, DE), BF16),
                pltpu.VMEM((8 * share, DE), BF16),
                pltpu.VMEM((32 * share, DX), F32),
                pltpu.VMEM((2, 32 * share, 4 * share), BF16),
                pltpu.VMEM((2, 32 * share, 4 * share), BF16),
                pltpu.VMEM((2, 8, 4 * share), F32),
                pltpu.VMEM((32 * share, DX), BF16),
                pltpu.VMEM((8 * share, DX), BF16),
                pltpu.VMEM((16 * share, DX), BF16),
                pltpu.VMEM((24, share, DX // 2), BF16),
                pltpu.VMEM((6, share, DX // 2), BF16),
                pltpu.VMEM((6, share, DX // 2), BF16),
                pltpu.VMEM((8, share, DX), BF16),
                pltpu.VMEM((16, share, 384), BF16),
                pltpu.VMEM((share, 384), F32),
                pltpu.VMEM((rows, 384), BF16),
                pltpu.VMEM((D, 256), F32),
                pltpu.VMEM((16, W + 16, 128), F32),
                pltpu.VMEM((16, W + 16, 128), F32),
                pltpu.VMEM((D, rows), BF16),
                pltpu.VMEM((D, rows), BF16),
            ]
            + [sem(n) for n in (16, 16, 64, 64, 8, 8, 4, 4, 32, 32, 8, 8, 16, 16, 16, 16)],
            compiler_params=pltpu.CompilerParams(
                collective_id=0, has_side_effects=True, vmem_limit_bytes=60 * 2**20
            ),
        )(enc_i, enc_t, w_i.T, w_t.T, dw_i.T, dw_t.T, sharpness, offset)

    in_specs = (
        P("dp", None),
        P("dp", None),
        P(None, "tensor"),
        P(None, "tensor"),
        P(None, "tensor"),
        P(None, "tensor"),
        P(),
        P(),
    )
    out_specs = (P("dp", "tensor"), P("dp", "tensor"))
    return jax.shard_map(local, mesh=mesh, in_specs=in_specs, out_specs=out_specs, check_vma=False)
```
